256 devices in a mesh: col: 16 (over z, core), tile: 16 (over y, x).
Axes of the slice: x: 4, y: 4, z: 8, core: 2. Of those that a mesh axis runs over, the one named last changes fastest.
Arguments:
- boundary: bfloat16 [16, 1024, 4, 1024], P('col', 'tile'), may hold values from -6 to 6
- row_tensors: bfloat16 [16, 4, 4, 4, 4], P('col'), may hold values from -3 to 3
- sketch_bond: bfloat16 [16, 1024, 1024], P('col', 'tile'), may hold values from -0.1875 to 0.1875
- sketch_phys: bfloat16 [16, 4, 4, 1024], P('col'), may hold values from -6 to 6
- edge_factor: bfloat16 [1024, 4, 1024], P('tile'), may hold values from -0.09375 to 0.09375
- closing: float32 [16, 4], P('col'), may hold values from 0.2 to 2
- left_edge: float32 [1024], replicated, may hold values from -6 to 6
Outputs:
- new_boundary: bfloat16 [16, 1024, 4, 1024], P('col', 'tile')
- envs: float32 [16, 1024], P('col', 'tile')
The draws below stay inside these ranges and needn't reach their ends.
All inputs are finite; a program needn't handle non-finite values.
Results may differ from the reference program's by a relative error of at most 0.012.
The reference program's roundings to bfloat16 on the way count: a program that leaves them out, or rounds other values in their place, can miss the bound.
Values may be sent and summed in bfloat16 or wider, within the bound.
A program may use at most 128 MiB of HBM per device.

```python
import math
import jax
import jax.numpy as jnp
from jax import lax

CHI = 1024
D = 4
COLS = 16


def block_levels(rng, extent, cuts, smallest, top_value):
    factor_of = 1.0
    for dim, shards_of in cuts:
        heights = jax.random.uniform(jax.random.fold_in(jax.random.fold_in(rng, 6), dim), (shards_of,), jnp.float32, smallest / len(cuts), top_value / len(cuts))
        factor_of = factor_of * jnp.repeat(jnp.exp(heights), extent[dim] // shards_of).reshape((-1,) + (1,) * (len(extent) - 1 - dim))
    return factor_of


def normal_values(rng, dims, spread, limit, split=(), held_as=jnp.bfloat16):
    array = spread * jax.random.normal(rng, dims, jnp.float32)
    if split:
        array = array * block_levels(rng, dims, split, -0.22, 0.18)
    return jnp.clip(array, -limit, limit).astype(held_as)


def setup_inputs(seed: int = 0) -> dict:
    streams_of = jax.random.split(jax.random.key(seed), 8)
    boundary = normal_values(streams_of[0], (COLS, CHI, D, CHI), 1.0, 6.0, ((0, 16), (1, 16)))
    row_tensors = normal_values(streams_of[1], (COLS, D, D, D, D), 0.5, 3.0, ((0, 16),))
    sketch_bond = normal_values(streams_of[2], (COLS, CHI, CHI), CHI ** -0.5, 0.1875, ((0, 16), (1, 16)))
    sketch_phys = normal_values(streams_of[3], (COLS, D, D, CHI), 1.0, 6.0, ((0, 16),))
    edge_factor = normal_values(streams_of[4], (CHI, D, CHI), (CHI * D) ** -0.5, 0.09375, ((0, 16),))
    closing = jnp.clip(jnp.exp(math.log(2.0) - 2.3025851 * jax.random.uniform(streams_of[5], (COLS, D), jnp.float32) ** block_levels(streams_of[5], (COLS, D), ((0, 16),), -0.2, 0.2)), 0.2, 2.0)
    left_edge = normal_values(streams_of[6], (CHI,), 1.0, 6.0, (), jnp.float32)
    return {"boundary": boundary, "row_tensors": row_tensors, "sketch_bond": sketch_bond, "sketch_phys": sketch_phys, "edge_factor": edge_factor, "closing": closing, "left_edge": left_edge}


GRAM_SHIFT = 0.001

def reference(boundary, row_tensors, sketch_bond, sketch_phys, edge_factor, closing, left_edge):
    highest = lax.Precision.HIGHEST
    left_basis = edge_factor
    sites = []
    for column in range(COLS):
        own_site = boundary[column].astype(jnp.float32)
        row_tensor = row_tensors[column].astype(jnp.float32)
        phys_map = jnp.einsum('lurd,ldk->urk', row_tensor, sketch_phys[column].astype(jnp.float32), precision=highest)
        sketched = jnp.einsum('bua,ka->buk', own_site, sketch_bond[column].astype(jnp.float32), precision=highest)
        range_rows = lax.optimization_barrier(jnp.sum(sketched[:, :, None, :] * phys_map[None], axis=1))
        range_flat = range_rows.reshape(CHI * D, CHI)
        gram = jnp.dot(range_flat.T, range_flat, precision=highest) + GRAM_SHIFT * jnp.eye(CHI, dtype=jnp.float32)
        lower_factor = jnp.linalg.cholesky(gram)
        basis = jax.scipy.linalg.solve_triangular(lower_factor, range_flat.T, lower=True).T
        basis = basis.astype(jnp.bfloat16).reshape(CHI, D, CHI)
        right_part = jnp.einsum('bua,brk->aurk', own_site, basis.astype(jnp.float32), precision=highest)
        absorbed = jnp.einsum('aurk,lurd->aldk', right_part, row_tensor, precision=highest)
        new_site = jnp.einsum('alc,aldk->kdc', left_basis.astype(jnp.float32), absorbed, precision=highest)
        sites.append(new_site.astype(jnp.bfloat16))
        left_basis = basis
    new_boundary = jnp.stack(sites)
    environment = left_edge
    envs = []
    for column in range(COLS):
        transfer = jnp.einsum('kdc,d->kc', new_boundary[column].astype(jnp.float32), closing[column], precision=highest).astype(jnp.bfloat16)
        weighted = jnp.dot(transfer.astype(jnp.float32), environment, precision=highest)
        environment = weighted * jnp.sqrt(jnp.float32(CHI)) / jnp.sqrt(jnp.sum(weighted * weighted) + 1e-06)
        envs.append(environment)
    return (new_boundary, jnp.stack(envs))
```

```python
import functools

import jax
import jax.numpy as jnp
from jax import lax
from jax.experimental import pallas as pl
from jax.experimental.pallas import tpu as pltpu
from jax.sharding import PartitionSpec as P

GRAM_SHIFT = 0.001
NB = 128
OWNER = 0
HIGHEST = lax.Precision.HIGHEST
MESH = pl.DeviceIdType.MESH
VMEM = pl.BlockSpec(memory_space=pltpu.VMEM)


def f32_dot(x, y, dims=(((1,), (0,)), ((), ()))):
    return lax.dot_general(x, y, dims, precision=HIGHEST, preferred_element_type=jnp.float32)


def factor_block(block, inv_ref):
    sub = lax.broadcasted_iota(jnp.int32, (8, NB), 0)
    lane = lax.broadcasted_iota(jnp.int32, (8, NB), 1)
    a0 = tuple(block[8 * i:8 * i + 8, :] for i in range(16))
    m0 = tuple((lane == sub + 8 * i).astype(jnp.float32) for i in range(16))

    def along(x, t):
        return jnp.broadcast_to(x[:, t:t + 1], (8, NB))

    def down(x, t):
        return jnp.broadcast_to(x[t:t + 1, :], (8, NB))

    def tree(terms):
        while len(terms) > 1:
            terms = [terms[i] + terms[i + 1] for i in range(0, len(terms), 2)]
        return terms[0]

    def group(count, g, carry):
        a, m = list(carry[0]), list(carry[1])
        p, n = a[0], m[0]
        c = [along(p, t) for t in range(8)]
        done = jnp.zeros((8, NB), jnp.float32)
        for s in range(8):
            here = sub == s
            pivot = down(c[s], s)
            inv = 1.0 / pivot
            nrow = down(n, s)
            done = jnp.where(here, nrow * lax.rsqrt(pivot), done)
            column = c[s]

            def step(x, row):
                row = row * inv
                return jnp.where(here, row, x - column * row)

            for t in range(s + 1, 8):
                c[t] = step(c[t], down(c[t], s))
            p = step(p, down(p, s))
            n = step(n, nrow)
        inv_ref[pl.ds(pl.multiple_of(g * 8, 8), 8), :] = done
        prow = [down(p, t) for t in range(8)]
        nrow = [down(n, t) for t in range(8)]
        for i in range(1, count):
            x = [along(a[i], t) for t in range(8)]
            a[i] = a[i] - tree([x[t] * prow[t] for t in range(8)])
            m[i] = m[i] - tree([x[t] * nrow[t] for t in range(8)])
        zero = jnp.zeros((8, NB), jnp.float32)
        return tuple(pltpu.roll(x, NB - 8, 1) for x in a[1:]) + (zero,), tuple(m[1:]) + (zero,)

    carry = (a0, m0)
    for lo in range(0, 16, 4):
        carry = (carry[0][:16 - lo], carry[1][:16 - lo])
        carry = lax.fori_loop(lo, lo + 4, functools.partial(group, 16 - lo), carry)


def basis_kernel(g_ref, r_ref, q_ref, s_ref, x_ref, inv_ref):
    n = g_ref.shape[0]
    eye = lax.broadcasted_iota(jnp.int32, (NB, NB), 0) == lax.broadcasted_iota(jnp.int32, (NB, NB), 1)
    for o in range(0, n, NB):
        e = o + NB
        src, rows = (g_ref, r_ref) if o == 0 else (s_ref, x_ref)
        factor_block(src[o:e, o:e] + jnp.where(eye, GRAM_SHIFT, 0.0), inv_ref)
        inv = inv_ref[...]
        q = f32_dot(rows[:, o:e], inv, (((1,), (1,)), ((), ())))
        q_ref[:, o:e] = q.astype(q_ref.dtype)
        if e == n:
            break
        upper = f32_dot(inv, src[o:e, e:])
        x_ref[:, e:] = rows[:, e:] - f32_dot(q, upper)
        for i in range(e, n, NB):
            s_ref[i:i + NB, i:] = src[i:i + NB, i:] - f32_dot(upper[:, i - e:i - e + NB].T, upper[:, i - e:])


def basis_of(gram, rows):
    n = gram.shape[0]
    return pl.pallas_call(
        basis_kernel,
        out_shape=jax.ShapeDtypeStruct(rows.shape, jnp.bfloat16),
        in_specs=[VMEM] * 2,
        out_specs=VMEM,
        scratch_shapes=[
            pltpu.VMEM((n, n), jnp.float32),
            pltpu.VMEM(rows.shape, jnp.float32),
            pltpu.VMEM((NB, NB), jnp.float32),
        ],
        compiler_params=pltpu.CompilerParams(vmem_limit_bytes=40 << 20),
        cost_estimate=pl.CostEstimate(flops=6 * 10**10, bytes_accessed=6 << 20, transcendentals=0),
    )(gram, rows)


def relay_kernel(cols, tiles, t_ref, edge_ref, env_ref, tall, across, arrived, stage, landed,
                 gather_send, gather_recv, chain_send, chain_recv, spread_send, spread_recv):
    col = lax.axis_index("col")
    tile = lax.axis_index("tile")
    share, width = t_ref.shape
    owner = tile == OWNER
    barrier = pltpu.get_barrier_semaphore()
    others = [t for t in range(tiles) if t != OWNER]

    def gather(slot, where):
        return pltpu.make_async_remote_copy(
            src_ref=t_ref, dst_ref=tall.at[slot], send_sem=gather_send, recv_sem=gather_recv.at[slot],
            device_id={"tile": where}, device_id_type=MESH)

    def spread(where):
        return pltpu.make_async_remote_copy(
            src_ref=stage, dst_ref=landed, send_sem=spread_send.at[where], recv_sem=spread_recv,
            device_id={"tile": where}, device_id_type=MESH)

    def chain(where):
        return pltpu.make_async_remote_copy(
            src_ref=stage, dst_ref=arrived, send_sem=chain_send, recv_sem=chain_recv,
            device_id={"col": where}, device_id_type=MESH)

    @pl.when(jnp.logical_not(owner))
    def _():
        pl.semaphore_signal(barrier, inc=1, device_id={"tile": OWNER}, device_id_type=MESH)
        pl.semaphore_wait(barrier, 1)
        gather(tile, OWNER).start()
        gather(tile, OWNER).wait_send()
        spread(OWNER).wait_recv()
        env_ref[...] = landed[...]

    @pl.when(owner)
    def _():
        for t in others:
            pl.semaphore_signal(barrier, inc=1, device_id={"tile": t}, device_id_type=MESH)

        for step in (1, cols - 1):
            pl.semaphore_signal(barrier, inc=1, device_id={"col": (col + step) % cols}, device_id_type=MESH)
        pl.semaphore_wait(barrier, len(others) + 2)
        tall[OWNER] = t_ref[...]
        per = NB // share
        for block in range(tiles // per):
            for t in range(block * per, block * per + per):
                if t != OWNER:
                    gather(t, t).wait_recv()
            rows = tall[block * per:block * per + per].reshape(NB, width).astype(jnp.float32)
            across[:, block * NB:block * NB + NB] = rows.T.astype(jnp.bfloat16)

        @pl.when(col == 0)
        def _():
            arrived[...] = edge_ref[...]

        @pl.when(col > 0)
        def _():
            chain(col).wait_recv()

        env = arrived[...]
        high = env.astype(jnp.bfloat16).astype(jnp.float32)
        middle = (env - high).astype(jnp.bfloat16).astype(jnp.float32)
        low = env - high - middle
        row = lax.broadcasted_iota(jnp.int32, (8, width), 0)
        parts = jnp.where(row == 0, high, jnp.where(row == 1, middle, jnp.where(row == 2, low, 0.0)))
        product = jnp.dot(parts.astype(jnp.bfloat16), across[...], preferred_element_type=jnp.float32)
        weighted = jnp.sum(product, axis=0, keepdims=True)
        squares = jnp.sum(weighted * weighted, axis=1, keepdims=True)
        stage[...] = weighted * (jnp.sqrt(jnp.float32(width)) / jnp.sqrt(squares + 1e-06))

        @pl.when(col < cols - 1)
        def _():
            chain(col + 1).start()

        for t in others:
            spread(t).start()
        env_ref[...] = stage[...]
        for t in others:
            spread(t).wait_send()

        @pl.when(col < cols - 1)
        def _():
            chain(col + 1).wait_send()


def relay(transfer_rows, left_edge, cols, tiles):
    share, width = transfer_rows.shape
    row = jax.ShapeDtypeStruct((1, width), jnp.float32)
    return pl.pallas_call(
        functools.partial(relay_kernel, cols, tiles),
        out_shape=row,
        in_specs=[VMEM] * 2,
        out_specs=VMEM,
        scratch_shapes=[
            pltpu.VMEM((tiles, share, width), jnp.bfloat16),
            pltpu.VMEM((width, width), jnp.bfloat16),
            pltpu.VMEM((1, width), jnp.float32),
            pltpu.VMEM((1, width), jnp.float32),
            pltpu.VMEM((1, width), jnp.float32),
            pltpu.SemaphoreType.DMA,
            pltpu.SemaphoreType.DMA((tiles,)),
            pltpu.SemaphoreType.DMA,
            pltpu.SemaphoreType.DMA,
            pltpu.SemaphoreType.DMA((tiles,)),
            pltpu.SemaphoreType.DMA,
        ],
        compiler_params=pltpu.CompilerParams(collective_id=1, has_side_effects=True, vmem_limit_bytes=32 << 20),
    )(transfer_rows, left_edge.reshape(1, width))


def passed_along(block, axis, distance):
    devices = range(lax.axis_size(axis))
    route = [(i - distance, i) for i in devices if i - distance in devices]
    return lax.ppermute(block, axis, route)


def local(boundary, row_tensors, sketch_bond, sketch_phys, edge_factor, closing, left_edge):
    highest = lax.Precision.HIGHEST
    own_site = boundary[0]
    row_tensor = row_tensors[0].astype(jnp.float32)
    bond_sketch = sketch_bond[0]
    phys_map = jnp.einsum(
        "lurd,ldk->urk", row_tensor, sketch_phys[0].astype(jnp.float32), precision=highest
    )
    local_rows, legs, width = own_site.shape
    sketched = jnp.einsum(
        "bua,ka->buk",
        own_site,
        lax.all_gather(bond_sketch, "tile", axis=0, tiled=True),
        preferred_element_type=jnp.float32,
    )
    range_rows = jnp.sum(sketched[:, :, None, :] * phys_map[None], axis=1)
    range_flat = range_rows.reshape(local_rows * legs, width)
    gram_local = jnp.dot(range_flat.T, range_flat, precision=highest)
    gram_total = lax.psum(gram_local, "tile")
    basis = basis_of(gram_total, range_flat).reshape(local_rows, legs, width)
    arrived = passed_along(basis, "col", 1)
    first_column = lax.axis_index("col") == 0
    left_basis = jnp.where(first_column, edge_factor, arrived)
    left_part = jnp.einsum(
        "alc,bua->club",
        lax.all_gather(left_basis, "tile", axis=0, tiled=True),
        own_site,
        preferred_element_type=jnp.float32,
    )
    left_absorbed = jnp.einsum("club,lurd->cdbr", left_part, row_tensor, precision=highest)
    new_site = lax.psum_scatter(
        jnp.einsum("cdbr,brk->kdc", left_absorbed, basis.astype(jnp.float32), precision=highest),
        "tile",
        scatter_dimension=0,
        tiled=True,
    )
    new_site = new_site.astype(jnp.bfloat16)
    transfer_rows = jnp.einsum(
        "kdc,d->kc", new_site.astype(jnp.float32), closing[0], precision=highest
    ).astype(jnp.bfloat16)
    env = relay(transfer_rows, left_edge, lax.axis_size("col"), lax.axis_size("tile"))
    share = transfer_rows.shape[0]
    env_local = lax.dynamic_slice(env, (0, lax.axis_index("tile") * share), (1, share))
    return (new_site[None], env_local)


def solution(mesh):
    in_specs = (
        P("col", "tile", None, None),
        P("col", None, None, None, None),
        P("col", "tile", None),
        P("col", None, None, None),
        P("tile", None, None),
        P("col", None),
        P(),
    )
    out_specs = (P("col", "tile", None, None), P("col", "tile"))
    return jax.shard_map(local, mesh=mesh, in_specs=in_specs, out_specs=out_specs, check_vma=False)
```

```python
import functools

import jax
import jax.numpy as jnp
from jax import lax
from jax.experimental import pallas as pl
from jax.experimental.pallas import tpu as pltpu
from jax.sharding import PartitionSpec as P

GRAM_SHIFT = 0.001
NB = 128
OWNER = 0
SIDE = 4
HIGHEST = lax.Precision.HIGHEST
MESH = pl.DeviceIdType.MESH
VMEM = pl.BlockSpec(memory_space=pltpu.VMEM)


def f32_dot(x, y, dims=(((1,), (0,)), ((), ()))):
    return lax.dot_general(x, y, dims, precision=HIGHEST, preferred_element_type=jnp.float32)


def factor_block(block, inv_ref):
    sub = lax.broadcasted_iota(jnp.int32, (8, NB), 0)
    lane = lax.broadcasted_iota(jnp.int32, (8, NB), 1)
    a0 = tuple(block[8 * i:8 * i + 8, :] for i in range(16))
    m0 = tuple((lane == sub + 8 * i).astype(jnp.float32) for i in range(16))

    def along(x, t):
        return jnp.broadcast_to(x[:, t:t + 1], (8, NB))

    def down(x, t):
        return jnp.broadcast_to(x[t:t + 1, :], (8, NB))

    def tree(terms):
        while len(terms) > 1:
            terms = [terms[i] + terms[i + 1] for i in range(0, len(terms), 2)]
        return terms[0]

    def group(count, g, carry):
        a, m = list(carry[0]), list(carry[1])
        p, n = a[0], m[0]
        c = [along(p, t) for t in range(8)]
        done = jnp.zeros((8, NB), jnp.float32)
        for s in range(8):
            here = sub == s
            pivot = down(c[s], s)
            inv = 1.0 / pivot
            nrow = down(n, s)
            done = jnp.where(here, nrow * lax.rsqrt(pivot), done)
            column = c[s]

            def step(x, row):
                row = row * inv
                return jnp.where(here, row, x - column * row)

            for t in range(s + 1, 8):
                c[t] = step(c[t], down(c[t], s))
            p = step(p, down(p, s))
            n = step(n, nrow)
        inv_ref[pl.ds(pl.multiple_of(g * 8, 8), 8), :] = done
        prow = [down(p, t) for t in range(8)]
        nrow = [down(n, t) for t in range(8)]
        for i in range(1, count):
            x = [along(a[i], t) for t in range(8)]
            a[i] = a[i] - tree([x[t] * prow[t] for t in range(8)])
            m[i] = m[i] - tree([x[t] * nrow[t] for t in range(8)])
        zero = jnp.zeros((8, NB), jnp.float32)
        return tuple(pltpu.roll(x, NB - 8, 1) for x in a[1:]) + (zero,), tuple(m[1:]) + (zero,)

    carry = (a0, m0)
    for lo in range(0, 16, 4):
        carry = (carry[0][:16 - lo], carry[1][:16 - lo])
        carry = lax.fori_loop(lo, lo + 4, functools.partial(group, 16 - lo), carry)


class Place:
    def __init__(self):
        tile = lax.axis_index("tile")
        self.tile = tile
        self.y, self.x = tile // SIDE, tile % SIDE

    def coordinate(self, axis):
        return self.x if axis == 0 else self.y

    def along(self, axis, index):
        return self.y * SIDE + index if axis == 0 else index * SIDE + self.x


def remote(src, dst, send, recv, where):
    return pltpu.make_async_remote_copy(
        src_ref=src, dst_ref=dst, send_sem=send, recv_sem=recv, device_id=where, device_id_type=MESH)


class LineGather:
    def __init__(self, place, axis, own, slot, sems, row=None):
        self.place, self.axis, self.own, self.slot, self.row = place, axis, own, slot, row
        self.send1, self.recv1, self.send2, self.recv2 = sems

    def first(self, s):
        place = self.place
        target = place.along(self.axis, (place.coordinate(self.axis) + s) % SIDE)
        return remote(self.own, self.slot(place.tile), self.send1.at[s - 1], self.recv1.at[s - 1], {"tile": target})

    def second(self, s, j):
        place = self.place
        other = 1 - self.axis
        target = place.along(other, (place.coordinate(other) + s) % SIDE)
        source = place.along(self.axis, (place.coordinate(self.axis) + SIDE - j) % SIDE)
        piece = self.own if j == 0 else self.slot(source)
        return remote(piece, self.slot(source), self.send2.at[s - 1, j], self.recv2.at[s - 1, j], {"tile": target})

    def start(self):
        for s in range(1, SIDE):
            self.first(s).start()

    def forward(self):
        for s in range(1, SIDE):
            self.second(s, 0).start()
        for j in range(1, SIDE):
            self.first(j).wait_recv()
            for s in range(1, SIDE):
                self.second(s, j).start()

    def finish(self):
        for s in range(1, SIDE):
            for j in range(SIDE):
                self.second(s, j).wait_recv()
        for s in range(1, SIDE):
            self.first(s).wait_send()
            for j in range(SIDE):
                self.second(s, j).wait_send()


LINE_SEMS = [
    pltpu.SemaphoreType.DMA((2, SIDE - 1)),
    pltpu.SemaphoreType.DMA((2, SIDE - 1)),
    pltpu.SemaphoreType.DMA((2, SIDE - 1, SIDE)),
    pltpu.SemaphoreType.DMA((2, SIDE - 1, SIDE)),
]


def front_kernel(b_ref, g_ref, phys_ref, q_ref, ball_ref, gall, r_ref, part, total, s_ref, inv_ref, *scratch):
    land, middle, land2, own = scratch[:2], scratch[2:4], scratch[4:6], scratch[6:8]
    sems = scratch[8:]
    g_sems, b_sems = sems[0:4], sems[4:8]
    rs1_send, rs1_recv, rs2_send, rs2_recv, ag1_send, ag1_recv, ag2_send, ag2_recv, here_sem = sems[8:]
    place = Place()
    legs, share, width = b_ref.shape
    barrier = pltpu.get_barrier_semaphore()
    for axis in (0, 1):
        for s in range(1, SIDE):
            target = place.along(axis, (place.coordinate(axis) + s) % SIDE)
            pl.semaphore_signal(barrier, inc=1, device_id={"tile": target}, device_id_type=MESH)
    pl.semaphore_wait(barrier, 2 * (SIDE - 1))

    half = share // 2
    sketch = [
        LineGather(
            place, h, g_ref.at[h * half:h * half + half],
            lambda tile, h=h: gall.at[pl.ds(pl.multiple_of(tile * share + h * half, half), half)],
            [x.at[h] for x in g_sems])
        for h in (0, 1)
    ]
    for gather in sketch:
        gather.start()
    mine = pl.multiple_of(place.tile * share, share)
    gall[pl.ds(mine, share), :] = g_ref[...]
    keep = pltpu.make_async_copy(b_ref, ball_ref.at[:, pl.ds(mine, share), :], here_sem)
    keep.start()
    for gather in sketch:
        gather.forward()
    for gather in sketch:
        gather.finish()

    for u in range(legs):
        sketched = lax.dot_general(
            b_ref[u], gall[...], (((1,), (1,)), ((), ())), preferred_element_type=jnp.float32)
        for r in range(legs):
            term = sketched * phys_ref[u * legs + r:u * legs + r + 1, :]
            rows = slice(r * share, r * share + share)
            r_ref[rows, :] = term if u == 0 else r_ref[rows, :] + term

    blocks = width // NB
    pairs = blocks // 2
    packed = NB * (blocks + 1)
    cut = NB * (pairs + 1)
    columns = ((0, cut), (cut, packed))

    def view(ref, i):
        lo = 0 if i < pairs else (i + 1) * NB
        return ref.at[i if i < pairs else blocks - 1 - i, :, lo:lo + (blocks - i) * NB]

    flipped = r_ref[...].T
    for i in range(blocks):
        view(part, i)[...] = f32_dot(flipped[i * NB:i * NB + NB, :], r_ref[:, i * NB:])

    strip = NB // SIDE

    def line(h):
        axis = h
        c1, c2 = place.coordinate(axis), place.coordinate(1 - axis)
        lo, hi = columns[h]
        return axis, c1, c2, slice(lo, hi)

    def rs1(h, s):
        axis, c1, c2, cols = line(h)
        p = (c1 + s) % SIDE
        return remote(part.at[p, :, cols], land[h].at[s - 1], rs1_send.at[h, s - 1], rs1_recv.at[h, s - 1],
                      {"tile": place.along(axis, p)})

    def rs2(h, s):
        axis, c1, c2, cols = line(h)
        p = (c2 + s) % SIDE
        return remote(middle[h].at[pl.ds(pl.multiple_of(p * strip, strip), strip)], land2[h].at[s - 1],
                      rs2_send.at[h, s - 1], rs2_recv.at[h, s - 1], {"tile": place.along(1 - axis, p)})

    def ag1(h, s):
        axis, c1, c2, cols = line(h)
        p = (c2 + s) % SIDE
        return remote(own[h], total.at[c1, pl.ds(pl.multiple_of(c2 * strip, strip), strip), cols],
                      ag1_send.at[h, s - 1], ag1_recv.at[h, s - 1], {"tile": place.along(1 - axis, p)})

    def ag2(h, s):
        axis, c1, c2, cols = line(h)
        p = (c1 + s) % SIDE
        return remote(total.at[c1, :, cols], total.at[c1, :, cols], ag2_send.at[h, s - 1], ag2_recv.at[h, s - 1],
                      {"tile": place.along(axis, p)})

    steps = range(1, SIDE)
    for h in (0, 1):
        for s in steps:
            rs1(h, s).start()
    for h in (0, 1):
        axis, c1, c2, cols = line(h)
        for s in steps:
            rs1(h, s).wait_recv()
        middle[h][...] = ((part[c1, :, cols] + land[h][0]) + (land[h][1] + land[h][2]))
        for s in steps:
            rs2(h, s).start()
    for h in (0, 1):
        axis, c1, c2, cols = line(h)
        for s in steps:
            rs2(h, s).wait_recv()
        strip_rows = pl.ds(pl.multiple_of(c2 * strip, strip), strip)
        own[h][...] = ((middle[h][strip_rows, :] + land2[h][0]) + (land2[h][1] + land2[h][2]))
        for s in steps:
            ag1(h, s).start()
        total[c1, strip_rows, cols] = own[h][...]
    for h in (0, 1):
        for s in steps:
            ag1(h, s).wait_recv()
        for s in steps:
            ag2(h, s).start()
    for h in (0, 1):
        for s in steps:
            ag2(h, s).wait_recv()
    for h in (0, 1):
        for s in steps:
            for copy in (rs1, rs2, ag1, ag2):
                copy(h, s).wait_send()

    two = legs // 2
    sites = [
        LineGather(
            place, h, b_ref.at[h * two:h * two + two],
            lambda tile, h=h: ball_ref.at[h * two:h * two + two, pl.ds(pl.multiple_of(tile * share, share), share), :],
            [x.at[h] for x in b_sems])
        for h in (0, 1)
    ]
    keep.wait()
    for gather in sites:
        gather.start()

    eye = lax.broadcasted_iota(jnp.int32, (NB, NB), 0) == lax.broadcasted_iota(jnp.int32, (NB, NB), 1)
    for i in range(blocks):
        o, e = i * NB, i * NB + NB
        src = view(total, 0) if i == 0 else s_ref.at[o:e, o:]
        factor_block(src[:, :NB] + jnp.where(eye, GRAM_SHIFT, 0.0), inv_ref)
        inv = inv_ref[...]
        q = f32_dot(r_ref[:, o:e], inv, (((1,), (1,)), ((), ())))
        q_ref[:, :, o:e] = q.reshape(legs, share, NB).astype(q_ref.dtype)
        if i == 1:
            for gather in sites:
                gather.forward()
        if e == width:
            break
        upper = f32_dot(inv, src[:, NB:])
        r_ref[:, e:] = r_ref[:, e:] - f32_dot(q, upper)
        for k in range(i + 1, blocks):
            before = view(total, k)[...] if i == 0 else s_ref[k * NB:k * NB + NB, k * NB:]
            lo = (k - i - 1) * NB
            s_ref[k * NB:k * NB + NB, k * NB:] = before - f32_dot(upper[:, lo:lo + NB].T, upper[:, lo:])
    for gather in sites:
        gather.finish()


def front(site, sketch, phys_map):
    legs, share, width = site.shape
    packed = width + NB
    cut = NB * (width // NB // 2 + 1)
    sizes = (cut, packed - cut)
    strip = NB // SIDE
    f32 = jnp.float32
    three = pltpu.SemaphoreType.DMA((2, SIDE - 1))
    return pl.pallas_call(
        front_kernel,
        out_shape=(
            jax.ShapeDtypeStruct((legs, share, width), jnp.bfloat16),
            jax.ShapeDtypeStruct((legs, width, width), jnp.bfloat16),
        ),
        in_specs=[VMEM] * 3,
        out_specs=(VMEM, pl.BlockSpec(memory_space=pl.ANY)),
        scratch_shapes=[
            pltpu.VMEM((width, width), jnp.bfloat16),
            pltpu.VMEM((legs * share, width), f32),
            pltpu.VMEM((SIDE, NB, packed), f32),
            pltpu.VMEM((SIDE, NB, packed), f32),
            pltpu.VMEM((width, width), f32),
            pltpu.VMEM((NB, NB), f32),
            *[pltpu.VMEM((SIDE - 1, NB, size), f32) for size in sizes],
            *[pltpu.VMEM((NB, size), f32) for size in sizes],
            *[pltpu.VMEM((SIDE - 1, strip, size), f32) for size in sizes],
            *[pltpu.VMEM((strip, size), f32) for size in sizes],
            *LINE_SEMS,
            *LINE_SEMS,
            *[three] * 8,
            pltpu.SemaphoreType.DMA,
        ],
        compiler_params=pltpu.CompilerParams(collective_id=0, has_side_effects=True, vmem_limit_bytes=48 << 20),
    )(site, sketch, phys_map)


def site_kernel(cols, tiles, q_ref, edge_ref, ball_ref, kron_ref, close_ref, out_ref, t_ref,
                ball, qall, lall, qt, x1, yh, yl, acc, osend, oall,
                ball_sem, keep_sem, q1_send, q1_recv, q2_send, q2_recv, l1_send, l1_recv, l2_send, l2_recv,
                o_send, o_recv):
    place = Place()
    col = lax.axis_index("col")
    legs, share, width = q_ref.shape
    wide = width // SIDE
    first, last = col == 0, col == cols - 1
    barrier = pltpu.get_barrier_semaphore()
    fetch = pltpu.make_async_copy(ball_ref, ball, ball_sem)
    fetch.start()

    def greet(where):
        pl.semaphore_signal(barrier, inc=1, device_id=where, device_id_type=MESH)

    for axis in (0, 1):
        for s in range(1, SIDE):
            greet({"tile": place.along(axis, (place.coordinate(axis) + s) % SIDE)})
    for i in range(SIDE):
        greet({"col": (col + cols - 1) % cols, "tile": place.along(0, i)})
    pl.semaphore_wait(barrier, 2 * (SIDE - 1) + SIDE)

    def chunk(ref, index):
        return ref.at[:, :, pl.ds(pl.multiple_of(index * wide, wide), wide)]

    def slot(ref, tile, count=1):
        return ref.at[:, pl.ds(pl.multiple_of(tile * share, share), count * share), :]

    def q1(s):
        target = (place.y + s) % SIDE
        return remote(chunk(q_ref, target), slot(qall, place.tile), q1_send.at[s - 1], q1_recv.at[s - 1],
                      {"tile": place.along(1, target)})

    def q2(s, j):
        source = place.along(1, (place.y + SIDE - j) % SIDE)
        piece = chunk(q_ref, place.y) if j == 0 else slot(qall, source)
        return remote(piece, slot(qall, source), q2_send.at[s - 1, j], q2_recv.at[s - 1, j],
                      {"tile": place.along(0, (place.x + s) % SIDE)})

    def l1(ref, s, column):
        target = (place.x + s) % SIDE
        return remote(chunk(ref, target), slot(lall, place.tile), l1_send.at[s], l1_recv.at[s],
                      {"col": column, "tile": place.along(0, target)})

    def edge1(s):
        target = (place.x + s) % SIDE
        return remote(chunk(edge_ref, target), slot(lall, place.tile), l2_send.at[SIDE - 2 + s], l1_recv.at[s],
                      {"tile": place.along(0, target)})

    def l2(s):
        rows = slot(lall, place.y * SIDE, SIDE)
        return remote(rows, rows, l2_send.at[s - 1], l2_recv.at[s - 1],
                      {"tile": place.along(1, (place.y + s) % SIDE)})

    def edge_own():
        return pltpu.make_async_copy(chunk(edge_ref, place.x), slot(lall, place.tile), l1_recv.at[0])

    steps = range(1, SIDE)
    for s in steps:
        q1(s).start()

    @pl.when(jnp.logical_not(last))
    def _():
        for s in range(SIDE):
            l1(q_ref, s, col + 1).start()

    @pl.when(first)
    def _():
        edge_own().start()
        for s in steps:
            edge1(s).start()

    own = pltpu.make_async_copy(chunk(q_ref, place.y), slot(qall, place.tile), keep_sem)
    own.start()
    for s in steps:
        q2(s, 0).start()
    for j in steps:
        q1(j).wait_recv()
        for s in steps:
            q2(s, j).start()

    @pl.when(first)
    def _():
        edge_own().wait()
        for s in steps:
            edge1(s).wait_recv()

    @pl.when(jnp.logical_not(first))
    def _():
        for s in range(SIDE):
            l1(q_ref, s, col).wait_recv()

    for s in steps:
        l2(s).start()
    own.wait()
    for s in steps:
        for j in range(SIDE):
            q2(s, j).wait_recv()
    for r in range(legs):
        qt[r * wide:r * wide + wide, :] = qall[r].astype(jnp.float32).T.astype(jnp.bfloat16)
    fetch.wait()

    groups = wide // 16
    for piece in range(width // wide):
        lanes = slice(piece * wide, piece * wide + wide)
        for u in range(legs):
            x1[:, u * wide:u * wide + wide] = jnp.dot(
                qt[...], ball[u, :, lanes], preferred_element_type=jnp.float32)

        @pl.loop(0, groups)
        def _(g):
            start = pl.multiple_of(g * 16, 16)
            stack = jnp.concatenate(
                [x1[pl.ds(pl.multiple_of(r * wide + start, 16), 16), u * wide:u * wide + wide]
                 for u in range(legs) for r in range(legs)], axis=0)
            high = stack.astype(jnp.bfloat16)
            low = (stack - high.astype(jnp.float32)).astype(jnp.bfloat16)
            y = (jnp.dot(kron_ref[...], high, preferred_element_type=jnp.float32)
                 + jnp.dot(kron_ref[...], low, preferred_element_type=jnp.float32))
            high = y.astype(jnp.bfloat16)
            low = (y - high.astype(jnp.float32)).astype(jnp.bfloat16)
            rows = pl.ds(pl.multiple_of(g * 64, 64), 64)
            for l in range(legs):
                yh[l, rows, :] = high[l * 64:l * 64 + 64]
                yl[l, rows, :] = low[l * 64:l * 64 + 64]

        if piece == 0:
            for s in steps:
                l2(s).wait_recv()
        for l in range(legs):
            left = lall[l, lanes, :]
            term = (jnp.dot(yh[l], left, preferred_element_type=jnp.float32)
                    + jnp.dot(yl[l], left, preferred_element_type=jnp.float32))
            acc[...] = term if piece == 0 and l == 0 else acc[...] + term

    def out(s):
        target = (place.x + s) % SIDE
        return remote(osend.at[pl.ds(pl.multiple_of(target * wide, wide), wide)],
                      oall.at[:, pl.ds(pl.multiple_of(place.x * wide, wide), wide)],
                      o_send.at[s - 1], o_recv.at[s - 1], {"tile": place.along(0, target)})

    osend[...] = acc[...].astype(jnp.bfloat16)
    for s in steps:
        out(s).start()
    mine = pl.multiple_of(place.x * wide, wide)
    oall[:, pl.ds(mine, wide)] = osend[pl.ds(mine, wide), :]
    for s in steps:
        out(s).wait_recv()
    out_ref[...] = oall[...]
    for g in range(share // 16):
        t = None
        for d in range(legs):
            term = oall[g * 64 + d * 16:g * 64 + d * 16 + 16, :].astype(jnp.float32) * close_ref[0, d]
            t = term if t is None else t + term
        t_ref[g * 16:g * 16 + 16, :] = t.astype(jnp.bfloat16)
    for s in steps:
        q1(s).wait_send()
        l2(s).wait_send()
        out(s).wait_send()
        for j in range(SIDE):
            q2(s, j).wait_send()

    @pl.when(first)
    def _():
        for s in steps:
            edge1(s).wait_send()

    @pl.when(jnp.logical_not(last))
    def _():
        for s in range(SIDE):
            l1(q_ref, s, col + 1).wait_send()


def new_site_of(basis, edge, whole_site, kron, closing, cols, tiles):
    legs, share, width = basis.shape
    wide = width // SIDE
    bf16, f32 = jnp.bfloat16, jnp.float32
    dma = pltpu.SemaphoreType.DMA
    return pl.pallas_call(
        functools.partial(site_kernel, cols, tiles),
        out_shape=(
            jax.ShapeDtypeStruct((legs * share, width), bf16),
            jax.ShapeDtypeStruct((share, width), bf16),
        ),
        in_specs=[VMEM, VMEM, pl.BlockSpec(memory_space=pl.ANY), VMEM, pl.BlockSpec(memory_space=pltpu.SMEM)],
        out_specs=(VMEM, VMEM),
        scratch_shapes=[
            pltpu.VMEM((legs, width, width), bf16),
            pltpu.VMEM((legs, width, wide), bf16),
            pltpu.VMEM((legs, width, wide), bf16),
            pltpu.VMEM((legs * wide, width), bf16),
            pltpu.VMEM((legs * wide, legs * wide), f32),
            pltpu.VMEM((legs, legs * wide, wide), bf16),
            pltpu.VMEM((legs, legs * wide, wide), bf16),
            pltpu.VMEM((legs * wide, wide), f32),
            pltpu.VMEM((legs * wide, wide), bf16),
            pltpu.VMEM((legs * share, width), bf16),
            dma, dma,
            dma((SIDE - 1,)), dma((SIDE - 1,)),
            dma((SIDE - 1, SIDE)), dma((SIDE - 1, SIDE)),
            dma((SIDE,)), dma((SIDE,)),
            dma((2 * SIDE - 2,)), dma((SIDE - 1,)),
            dma((SIDE - 1,)), dma((SIDE - 1,)),
        ],
        compiler_params=pltpu.CompilerParams(collective_id=2, has_side_effects=True, vmem_limit_bytes=56 << 20),
    )(basis, edge, whole_site, kron, closing)


def relay_kernel(cols, tiles, t_ref, edge_ref, env_ref, tall, across, arrived, stage, landed,
                 gather_send, gather_recv, chain_send, chain_recv, spread_send, spread_recv):
    col = lax.axis_index("col")
    tile = lax.axis_index("tile")
    share, width = t_ref.shape
    owner = tile == OWNER
    barrier = pltpu.get_barrier_semaphore()
    others = [t for t in range(tiles) if t != OWNER]

    def gather(slot, where):
        return pltpu.make_async_remote_copy(
            src_ref=t_ref, dst_ref=tall.at[slot], send_sem=gather_send, recv_sem=gather_recv.at[slot],
            device_id={"tile": where}, device_id_type=MESH)

    def spread(where):
        return pltpu.make_async_remote_copy(
            src_ref=stage, dst_ref=landed, send_sem=spread_send.at[where], recv_sem=spread_recv,
            device_id={"tile": where}, device_id_type=MESH)

    def chain(where):
        return pltpu.make_async_remote_copy(
            src_ref=stage, dst_ref=arrived, send_sem=chain_send, recv_sem=chain_recv,
            device_id={"col": where}, device_id_type=MESH)

    @pl.when(jnp.logical_not(owner))
    def _():
        pl.semaphore_signal(barrier, inc=1, device_id={"tile": OWNER}, device_id_type=MESH)
        pl.semaphore_wait(barrier, 1)
        gather(tile, OWNER).start()
        gather(tile, OWNER).wait_send()
        spread(OWNER).wait_recv()
        env_ref[...] = landed[...]

    @pl.when(owner)
    def _():
        for t in others:
            pl.semaphore_signal(barrier, inc=1, device_id={"tile": t}, device_id_type=MESH)

        for step in (1, cols - 1):
            pl.semaphore_signal(barrier, inc=1, device_id={"col": (col + step) % cols}, device_id_type=MESH)
        pl.semaphore_wait(barrier, len(others) + 2)
        tall[OWNER] = t_ref[...]
        per = NB // share
        for block in range(tiles // per):
            for t in range(block * per, block * per + per):
                if t != OWNER:
                    gather(t, t).wait_recv()
            rows = tall[block * per:block * per + per].reshape(NB, width).astype(jnp.float32)
            across[:, block * NB:block * NB + NB] = rows.T.astype(jnp.bfloat16)

        @pl.when(col == 0)
        def _():
            arrived[...] = edge_ref[...]

        @pl.when(col > 0)
        def _():
            chain(col).wait_recv()

        env = arrived[...]
        high = env.astype(jnp.bfloat16).astype(jnp.float32)
        middle = (env - high).astype(jnp.bfloat16).astype(jnp.float32)
        low = env - high - middle
        row = lax.broadcasted_iota(jnp.int32, (8, width), 0)
        parts = jnp.where(row == 0, high, jnp.where(row == 1, middle, jnp.where(row == 2, low, 0.0)))
        product = jnp.dot(parts.astype(jnp.bfloat16), across[...], preferred_element_type=jnp.float32)
        weighted = jnp.sum(product, axis=0, keepdims=True)
        squares = jnp.sum(weighted * weighted, axis=1, keepdims=True)
        stage[...] = weighted * (jnp.sqrt(jnp.float32(width)) / jnp.sqrt(squares + 1e-06))

        @pl.when(col < cols - 1)
        def _():
            chain(col + 1).start()

        for t in others:
            spread(t).start()
        env_ref[...] = stage[...]
        for t in others:
            spread(t).wait_send()

        @pl.when(col < cols - 1)
        def _():
            chain(col + 1).wait_send()


def relay(transfer_rows, left_edge, cols, tiles):
    share, width = transfer_rows.shape
    row = jax.ShapeDtypeStruct((1, width), jnp.float32)
    return pl.pallas_call(
        functools.partial(relay_kernel, cols, tiles),
        out_shape=row,
        in_specs=[VMEM] * 2,
        out_specs=VMEM,
        scratch_shapes=[
            pltpu.VMEM((tiles, share, width), jnp.bfloat16),
            pltpu.VMEM((width, width), jnp.bfloat16),
            pltpu.VMEM((1, width), jnp.float32),
            pltpu.VMEM((1, width), jnp.float32),
            pltpu.VMEM((1, width), jnp.float32),
            pltpu.SemaphoreType.DMA,
            pltpu.SemaphoreType.DMA((tiles,)),
            pltpu.SemaphoreType.DMA,
            pltpu.SemaphoreType.DMA,
            pltpu.SemaphoreType.DMA((tiles,)),
            pltpu.SemaphoreType.DMA,
        ],
        compiler_params=pltpu.CompilerParams(collective_id=1, has_side_effects=True, vmem_limit_bytes=32 << 20),
    )(transfer_rows, left_edge.reshape(1, width))


def local(boundary, row_tensors, sketch_bond, sketch_phys, edge_factor, closing, left_edge):
    cols, tiles = lax.axis_size("col"), lax.axis_size("tile")
    share, legs, width = boundary.shape[1:]
    row_tensor = row_tensors[0]
    phys_map = jnp.einsum(
        "lurd,ldk->urk", row_tensor.astype(jnp.float32), sketch_phys[0].astype(jnp.float32), precision=HIGHEST
    )
    basis, whole_site = front(
        boundary[0].transpose(1, 0, 2), sketch_bond[0], phys_map.reshape(legs * legs, width))
    kron = jnp.einsum("lurd,st->ldsurt", row_tensor.astype(jnp.float32), jnp.eye(16, dtype=jnp.float32),
                      precision=HIGHEST)
    kron = kron.reshape(16 * legs * legs, 16 * legs * legs).astype(jnp.bfloat16)
    rows, transfer_rows = new_site_of(
        basis, edge_factor.transpose(1, 0, 2), whole_site, kron, closing, cols, tiles)
    new_site = rows.reshape(share // 16, legs, 16, width).transpose(0, 2, 1, 3).reshape(share, legs, width)
    env = relay(transfer_rows, left_edge, cols, tiles)
    env_local = lax.dynamic_slice(env, (0, lax.axis_index("tile") * share), (1, share))
    return (new_site[None], env_local)


def solution(mesh):
    in_specs = (
        P("col", "tile", None, None),
        P("col", None, None, None, None),
        P("col", "tile", None),
        P("col", None, None, None),
        P("tile", None, None),
        P("col", None),
        P(),
    )
    out_specs = (P("col", "tile", None, None), P("col", "tile"))
    return jax.shard_map(local, mesh=mesh, in_specs=in_specs, out_specs=out_specs, check_vma=False)
```

```python
import functools

import jax
import jax.numpy as jnp
from jax import lax
from jax.experimental import pallas as pl
from jax.experimental.pallas import tpu as pltpu
from jax.sharding import PartitionSpec as P

GRAM_SHIFT = 0.001
NB = 128
OWNER = 0
SIDE = 4
HIGHEST = lax.Precision.HIGHEST
MESH = pl.DeviceIdType.MESH
VMEM = pl.BlockSpec(memory_space=pltpu.VMEM)


def f32_dot(x, y, dims=(((1,), (0,)), ((), ()))):
    return lax.dot_general(x, y, dims, precision=HIGHEST, preferred_element_type=jnp.float32)


def factor_block(block, inv_ref):
    sub = lax.broadcasted_iota(jnp.int32, (8, NB), 0)
    lane = lax.broadcasted_iota(jnp.int32, (8, NB), 1)
    a0 = tuple(block[8 * i:8 * i + 8, :] for i in range(16))
    m0 = tuple((lane == sub + 8 * i).astype(jnp.float32) for i in range(16))

    def along(x, t):
        return jnp.broadcast_to(x[:, t:t + 1], (8, NB))

    def down(x, t):
        return jnp.broadcast_to(x[t:t + 1, :], (8, NB))

    def tree(terms):
        while len(terms) > 1:
            terms = [terms[i] + terms[i + 1] for i in range(0, len(terms), 2)]
        return terms[0]

    def group(count, g, carry):
        a, m, c = list(carry[0]), list(carry[1]), list(carry[2])
        p, n = a[0], m[0]
        done = jnp.zeros((8, NB), jnp.float32)
        for s in range(8):
            here = sub == s
            pivot = down(c[s], s)
            inv = 1.0 / pivot
            nrow = down(n, s)
            done = jnp.where(here, nrow * lax.rsqrt(pivot), done)
            column = c[s]

            def step(x, row):
                row = row * inv
                return jnp.where(here, row, x - column * row)

            for t in range(s + 1, 8):
                c[t] = step(c[t], down(c[t], s))
            p = step(p, down(p, s))
            n = step(n, nrow)
        inv_ref[pl.ds(pl.multiple_of(g * 8, 8), 8), :] = done
        prow = [down(p, t) for t in range(8)]
        nrow = [down(n, t) for t in range(8)]
        for i in range(1, count):
            x = [along(a[i], t) for t in range(8)]
            a[i] = a[i] - tree([x[t] * prow[t] for t in range(8)])
            m[i] = m[i] - tree([x[t] * nrow[t] for t in range(8)])
            if i == 1:
                c = [along(a[1], 8 + t) for t in range(8)]
        zero = jnp.zeros((8, NB), jnp.float32)
        return tuple(pltpu.roll(x, NB - 8, 1) for x in a[1:]) + (zero,), tuple(m[1:]) + (zero,), tuple(c)

    carry = (a0, m0, tuple(along(a0[0], t) for t in range(8)))
    for lo in range(0, 16, 4):
        carry = (carry[0][:16 - lo], carry[1][:16 - lo], carry[2])
        carry = lax.fori_loop(lo, lo + 4, functools.partial(group, 16 - lo), carry)


class Place:
    def __init__(self):
        tile = lax.axis_index("tile")
        self.tile = tile
        self.y, self.x = tile // SIDE, tile % SIDE

    def coordinate(self, axis):
        return self.x if axis == 0 else self.y

    def along(self, axis, index):
        return self.y * SIDE + index if axis == 0 else index * SIDE + self.x


def remote(src, dst, send, recv, where):
    return pltpu.make_async_remote_copy(
        src_ref=src, dst_ref=dst, send_sem=send, recv_sem=recv, device_id=where, device_id_type=MESH)


class LineGather:
    def __init__(self, place, axis, own, slot, sems, row=None):
        self.place, self.axis, self.own, self.slot, self.row = place, axis, own, slot, row
        self.send1, self.recv1, self.send2, self.recv2 = sems

    def first(self, s):
        place = self.place
        target = place.along(self.axis, (place.coordinate(self.axis) + s) % SIDE)
        return remote(self.own, self.slot(place.tile), self.send1.at[s - 1], self.recv1.at[s - 1], {"tile": target})

    def second(self, s, j):
        place = self.place
        other = 1 - self.axis
        target = place.along(other, (place.coordinate(other) + s) % SIDE)
        source = place.along(self.axis, (place.coordinate(self.axis) + SIDE - j) % SIDE)
        piece = self.own if j == 0 else self.slot(source)
        return remote(piece, self.slot(source), self.send2.at[s - 1, j], self.recv2.at[s - 1, j], {"tile": target})

    def start(self):
        for s in range(1, SIDE):
            self.first(s).start()

    def forward(self):
        for s in range(1, SIDE):
            self.second(s, 0).start()
        for j in range(1, SIDE):
            self.first(j).wait_recv()
            for s in range(1, SIDE):
                self.second(s, j).start()

    def finish(self):
        for s in range(1, SIDE):
            for j in range(SIDE):
                self.second(s, j).wait_recv()
        for s in range(1, SIDE):
            self.first(s).wait_send()
            for j in range(SIDE):
                self.second(s, j).wait_send()


LINE_SEMS = [
    pltpu.SemaphoreType.DMA((2, SIDE - 1)),
    pltpu.SemaphoreType.DMA((2, SIDE - 1)),
    pltpu.SemaphoreType.DMA((2, SIDE - 1, SIDE)),
    pltpu.SemaphoreType.DMA((2, SIDE - 1, SIDE)),
]


def front_kernel(b_ref, g_ref, phys_ref, q_ref, ball_ref, gall, r_ref, part, total, s_ref, inv_ref, *scratch):
    land, middle, land2, own = scratch[:2], scratch[2:4], scratch[4:6], scratch[6:8]
    sems = scratch[8:]
    g_sems, b_sems = sems[0:4], sems[4:8]
    rs1_send, rs1_recv, rs2_send, rs2_recv, ag1_send, ag1_recv, ag2_send, ag2_recv, here_sem = sems[8:]
    place = Place()
    legs, share, width = b_ref.shape
    barrier = pltpu.get_barrier_semaphore()
    for axis in (0, 1):
        for s in range(1, SIDE):
            target = place.along(axis, (place.coordinate(axis) + s) % SIDE)
            pl.semaphore_signal(barrier, inc=1, device_id={"tile": target}, device_id_type=MESH)
    pl.semaphore_wait(barrier, 2 * (SIDE - 1))

    half = share // 2
    sketch = [
        LineGather(
            place, h, g_ref.at[h * half:h * half + half],
            lambda tile, h=h: gall.at[pl.ds(pl.multiple_of(tile * share + h * half, half), half)],
            [x.at[h] for x in g_sems])
        for h in (0, 1)
    ]
    for gather in sketch:
        gather.start()
    mine = pl.multiple_of(place.tile * share, share)
    gall[pl.ds(mine, share), :] = g_ref[...]
    keep = pltpu.make_async_copy(b_ref, ball_ref.at[:, pl.ds(mine, share), :], here_sem)
    keep.start()
    for gather in sketch:
        gather.forward()
    for gather in sketch:
        gather.finish()

    two = legs // 2
    sites = [
        LineGather(
            place, h, b_ref.at[h * two:h * two + two],
            lambda tile, h=h: ball_ref.at[h * two:h * two + two, pl.ds(pl.multiple_of(tile * share, share), share), :],
            [x.at[h] for x in b_sems])
        for h in (0, 1)
    ]
    keep.wait()
    for gather in sites:
        gather.start()

    for u in range(legs):
        sketched = lax.dot_general(
            b_ref[u], gall[...], (((1,), (1,)), ((), ())), preferred_element_type=jnp.float32)
        for r in range(legs):
            term = sketched * phys_ref[u * legs + r:u * legs + r + 1, :]
            rows = slice(r * share, r * share + share)
            r_ref[rows, :] = term if u == 0 else r_ref[rows, :] + term

    blocks = width // NB
    pairs = blocks // 2
    packed = NB * (blocks + 1)
    cut = NB * (pairs + 1)
    columns = ((0, cut), (cut, packed))

    def view(ref, i):
        lo = 0 if i < pairs else (i + 1) * NB
        return ref.at[i if i < pairs else blocks - 1 - i, :, lo:lo + (blocks - i) * NB]

    flipped = r_ref[...].T
    for i in range(blocks):
        view(part, i)[...] = f32_dot(flipped[i * NB:i * NB + NB, :], r_ref[:, i * NB:])

    strip = NB // SIDE

    def line(h):
        axis = h
        c1, c2 = place.coordinate(axis), place.coordinate(1 - axis)
        lo, hi = columns[h]
        return axis, c1, c2, slice(lo, hi)

    def rs1(h, s):
        axis, c1, c2, cols = line(h)
        p = (c1 + s) % SIDE
        return remote(part.at[p, :, cols], land[h].at[s - 1], rs1_send.at[h, s - 1], rs1_recv.at[h, s - 1],
                      {"tile": place.along(axis, p)})

    def rs2(h, s):
        axis, c1, c2, cols = line(h)
        p = (c2 + s) % SIDE
        return remote(middle[h].at[pl.ds(pl.multiple_of(p * strip, strip), strip)], land2[h].at[s - 1],
                      rs2_send.at[h, s - 1], rs2_recv.at[h, s - 1], {"tile": place.along(1 - axis, p)})

    def ag1(h, s):
        axis, c1, c2, cols = line(h)
        p = (c2 + s) % SIDE
        return remote(own[h], total.at[c1, pl.ds(pl.multiple_of(c2 * strip, strip), strip), cols],
                      ag1_send.at[h, s - 1], ag1_recv.at[h, s - 1], {"tile": place.along(1 - axis, p)})

    def ag2(h, s):
        axis, c1, c2, cols = line(h)
        p = (c1 + s) % SIDE
        return remote(total.at[c1, :, cols], total.at[c1, :, cols], ag2_send.at[h, s - 1], ag2_recv.at[h, s - 1],
                      {"tile": place.along(axis, p)})

    steps = range(1, SIDE)
    for h in (0, 1):
        for s in steps:
            rs1(h, s).start()
    for h in (0, 1):
        axis, c1, c2, cols = line(h)
        for s in steps:
            rs1(h, s).wait_recv()
        middle[h][...] = ((part[c1, :, cols] + land[h][0]) + (land[h][1] + land[h][2]))
        for s in steps:
            rs2(h, s).start()
    for h in (0, 1):
        axis, c1, c2, cols = line(h)
        for s in steps:
            rs2(h, s).wait_recv()
        strip_rows = pl.ds(pl.multiple_of(c2 * strip, strip), strip)
        own[h][...] = ((middle[h][strip_rows, :] + land2[h][0]) + (land2[h][1] + land2[h][2]))
        for s in steps:
            ag1(h, s).start()
        total[c1, strip_rows, cols] = own[h][...]
    for h in (0, 1):
        for s in steps:
            ag1(h, s).wait_recv()
        for s in steps:
            ag2(h, s).start()
    for h in (0, 1):
        for s in steps:
            ag2(h, s).wait_recv()
    for h in (0, 1):
        for s in steps:
            for copy in (rs1, rs2, ag1, ag2):
                copy(h, s).wait_send()

    for gather in sites:
        gather.forward()

    eye = lax.broadcasted_iota(jnp.int32, (NB, NB), 0) == lax.broadcasted_iota(jnp.int32, (NB, NB), 1)
    for i in range(blocks):
        o, e = i * NB, i * NB + NB
        src = view(total, 0) if i == 0 else s_ref.at[o:e, o:]
        factor_block(src[:, :NB] + jnp.where(eye, GRAM_SHIFT, 0.0), inv_ref)
        inv = inv_ref[...]
        q = f32_dot(r_ref[:, o:e], inv, (((1,), (1,)), ((), ())))
        q_ref[:, :, o:e] = q.reshape(legs, share, NB).astype(q_ref.dtype)
        if e == width:
            break
        upper = f32_dot(inv, src[:, NB:])
        r_ref[:, e:] = r_ref[:, e:] - f32_dot(q, upper)
        for k in range(i + 1, blocks):
            before = view(total, k)[...] if i == 0 else s_ref[k * NB:k * NB + NB, k * NB:]
            lo = (k - i - 1) * NB
            s_ref[k * NB:k * NB + NB, k * NB:] = before - f32_dot(upper[:, lo:lo + NB].T, upper[:, lo:])
    for gather in sites:
        gather.finish()


def front(site, sketch, phys_map):
    legs, share, width = site.shape
    packed = width + NB
    cut = NB * (width // NB // 2 + 1)
    sizes = (cut, packed - cut)
    strip = NB // SIDE
    f32 = jnp.float32
    three = pltpu.SemaphoreType.DMA((2, SIDE - 1))
    return pl.pallas_call(
        front_kernel,
        out_shape=(
            jax.ShapeDtypeStruct((legs, share, width), jnp.bfloat16),
            jax.ShapeDtypeStruct((legs, width, width), jnp.bfloat16),
        ),
        in_specs=[VMEM] * 3,
        out_specs=(VMEM, pl.BlockSpec(memory_space=pl.ANY)),
        scratch_shapes=[
            pltpu.VMEM((width, width), jnp.bfloat16),
            pltpu.VMEM((legs * share, width), f32),
            pltpu.VMEM((SIDE, NB, packed), f32),
            pltpu.VMEM((SIDE, NB, packed), f32),
            pltpu.VMEM((width, width), f32),
            pltpu.VMEM((NB, NB), f32),
            *[pltpu.VMEM((SIDE - 1, NB, size), f32) for size in sizes],
            *[pltpu.VMEM((NB, size), f32) for size in sizes],
            *[pltpu.VMEM((SIDE - 1, strip, size), f32) for size in sizes],
            *[pltpu.VMEM((strip, size), f32) for size in sizes],
            *LINE_SEMS,
            *LINE_SEMS,
            *[three] * 8,
            pltpu.SemaphoreType.DMA,
        ],
        compiler_params=pltpu.CompilerParams(collective_id=0, has_side_effects=True, vmem_limit_bytes=48 << 20),
    )(site, sketch, phys_map)


def site_kernel(cols, tiles, q_ref, edge_ref, ball_ref, kron_ref, close_ref, first_ref, out_ref, env_ref,
                ball, qall, lall, qt, x1, yh, yl, acc, osend, oall, tsend, across, arrived, stage, landed,
                gather_send, gather_recv, chain_send, chain_recv, spread_send, spread_recv,
                ball_sem, keep_sem, q1_send, q1_recv, q2_send, q2_recv, l1_send, l1_recv, l2_send, l2_recv,
                o_send, o_recv):
    place = Place()
    col = lax.axis_index("col")
    legs, share, width = q_ref.shape
    wide = width // SIDE
    first, last = col == 0, col == cols - 1
    barrier = pltpu.get_barrier_semaphore()
    fetch = pltpu.make_async_copy(ball_ref, ball, ball_sem)
    fetch.start()

    def greet(where):
        pl.semaphore_signal(barrier, inc=1, device_id=where, device_id_type=MESH)

    for s in range(1, tiles):
        greet({"tile": (place.tile + s) % tiles})
    for i in range(SIDE):
        greet({"col": (col + cols - 1) % cols, "tile": place.along(0, i)})
    pl.semaphore_wait(barrier, tiles - 1 + SIDE)

    def chunk(ref, index):
        return ref.at[:, :, pl.ds(pl.multiple_of(index * wide, wide), wide)]

    def slot(ref, tile, count=1):
        return ref.at[:, pl.ds(pl.multiple_of(tile * share, share), count * share), :]

    def q1(s):
        target = (place.y + s) % SIDE
        return remote(chunk(q_ref, target), slot(qall, place.tile), q1_send.at[s - 1], q1_recv.at[s - 1],
                      {"tile": place.along(1, target)})

    def q2(s, j):
        source = place.along(1, (place.y + SIDE - j) % SIDE)
        piece = chunk(q_ref, place.y) if j == 0 else slot(qall, source)
        return remote(piece, slot(qall, source), q2_send.at[s - 1, j], q2_recv.at[s - 1, j],
                      {"tile": place.along(0, (place.x + s) % SIDE)})

    def l1(ref, s, column):
        target = (place.x + s) % SIDE
        return remote(chunk(ref, target), slot(lall, place.tile), l1_send.at[s], l1_recv.at[s],
                      {"col": column, "tile": place.along(0, target)})

    def edge1(s):
        target = (place.x + s) % SIDE
        return remote(chunk(edge_ref, target), slot(lall, place.tile), l2_send.at[SIDE - 2 + s], l1_recv.at[s],
                      {"tile": place.along(0, target)})

    def l2(s):
        rows = slot(lall, place.y * SIDE, SIDE)
        return remote(rows, rows, l2_send.at[s - 1], l2_recv.at[s - 1],
                      {"tile": place.along(1, (place.y + s) % SIDE)})

    def edge_own():
        return pltpu.make_async_copy(chunk(edge_ref, place.x), slot(lall, place.tile), l1_recv.at[0])

    steps = range(1, SIDE)
    for s in steps:
        q1(s).start()

    @pl.when(jnp.logical_not(last))
    def _():
        for s in range(SIDE):
            l1(q_ref, s, col + 1).start()

    @pl.when(first)
    def _():
        edge_own().start()
        for s in steps:
            edge1(s).start()

    own = pltpu.make_async_copy(chunk(q_ref, place.y), slot(qall, place.tile), keep_sem)
    own.start()
    for s in steps:
        q2(s, 0).start()
    for j in steps:
        q1(j).wait_recv()
        for s in steps:
            q2(s, j).start()

    @pl.when(first)
    def _():
        edge_own().wait()
        for s in steps:
            edge1(s).wait_recv()

    @pl.when(jnp.logical_not(first))
    def _():
        for s in range(SIDE):
            l1(q_ref, s, col).wait_recv()

    for s in steps:
        l2(s).start()
    own.wait()
    for s in steps:
        for j in range(SIDE):
            q2(s, j).wait_recv()
    for r in range(legs):
        qt[r * wide:r * wide + wide, :] = qall[r].astype(jnp.float32).T.astype(jnp.bfloat16)
    fetch.wait()

    groups = wide // 16
    acc[...] = jnp.zeros_like(acc)

    @pl.loop(0, width // wide)
    def _(piece):
        lanes = pl.ds(pl.multiple_of(piece * wide, wide), wide)
        for u in range(legs):
            x1[:, u * wide:u * wide + wide] = jnp.dot(
                qt[...], ball[u, :, lanes], preferred_element_type=jnp.float32)

        @pl.loop(0, groups // 2)
        def _(pair):
            for g in (pair * 2, pair * 2 + 1):
                start = pl.multiple_of(g * 16, 16)
                stack = jnp.concatenate(
                    [x1[pl.ds(pl.multiple_of(r * wide + start, 16), 16), u * wide:u * wide + wide]
                     for u in range(legs) for r in range(legs)], axis=0)
                high = stack.astype(jnp.bfloat16)
                low = (stack - high.astype(jnp.float32)).astype(jnp.bfloat16)
                y = (jnp.dot(kron_ref[...], high, preferred_element_type=jnp.float32)
                     + jnp.dot(kron_ref[...], low, preferred_element_type=jnp.float32))
                high = y.astype(jnp.bfloat16)
                low = (y - high.astype(jnp.float32)).astype(jnp.bfloat16)
                rows = pl.ds(pl.multiple_of(g * 64, 64), 64)
                for l in range(legs):
                    yh[l, rows, :] = high[l * 64:l * 64 + 64]
                    yl[l, rows, :] = low[l * 64:l * 64 + 64]

        @pl.when(piece == 0)
        def _():
            for s in steps:
                l2(s).wait_recv()

        for l in range(legs):
            left = lall[l, lanes, :]
            term = (jnp.dot(yh[l], left, preferred_element_type=jnp.float32)
                    + jnp.dot(yl[l], left, preferred_element_type=jnp.float32))
            acc[...] = acc[...] + term

    def out(s):
        target = (place.x + s) % SIDE
        return remote(osend.at[pl.ds(pl.multiple_of(target * wide, wide), wide)],
                      oall.at[:, pl.ds(pl.multiple_of(place.x * wide, wide), wide)],
                      o_send.at[s - 1], o_recv.at[s - 1], {"tile": place.along(0, target)})

    owner = place.tile == OWNER
    others = [t for t in range(tiles) if t != OWNER]
    block = (pl.ds(pl.multiple_of(place.x * wide, wide), wide), pl.ds(pl.multiple_of(place.y * wide, wide), wide))

    def gather(slot):
        return remote(tsend, across.at[block], gather_send, gather_recv.at[slot], {"tile": OWNER})

    def spread(where):
        return remote(stage, landed, spread_send.at[where], spread_recv, {"tile": where})

    def chain(where):
        return remote(stage, arrived, chain_send, chain_recv, {"col": where})

    def scale_of(raw):
        squares = jnp.sum(raw * raw, axis=1, keepdims=True)
        return jnp.sqrt(jnp.float32(width)) / jnp.sqrt(squares + 1e-06)

    osend[...] = acc[...].astype(jnp.bfloat16)
    rows = []
    for g in range(groups):
        t = None
        for d in range(legs):
            lo = (g * legs + d) * 16
            term = osend[lo:lo + 16, :].astype(jnp.float32) * close_ref[0, d]
            t = term if t is None else t + term
        rows.append(t)
    transfer = jnp.concatenate(rows, axis=0).astype(jnp.bfloat16).astype(jnp.float32)
    tsend[...] = transfer.T.astype(jnp.bfloat16)

    @pl.when(jnp.logical_not(owner))
    def _():
        gather(place.tile).start()

    for s in steps:
        out(s).start()
    mine = pl.multiple_of(place.x * wide, wide)
    oall[:, pl.ds(mine, wide)] = osend[pl.ds(mine, wide), :]

    @pl.when(owner)
    def _():
        across[block] = tsend[...]
        for t in others:
            gather(t).wait_recv()

        @pl.when(first)
        def _():
            arrived[...] = first_ref[...]

        @pl.when(jnp.logical_not(first))
        def _():
            chain(col).wait_recv()

        raw = arrived[...]
        high = raw.astype(jnp.bfloat16).astype(jnp.float32)
        middle = (raw - high).astype(jnp.bfloat16).astype(jnp.float32)
        low = raw - high - middle
        row = lax.broadcasted_iota(jnp.int32, (8, width), 0)
        parts = jnp.where(row == 0, high, jnp.where(row == 1, middle, jnp.where(row == 2, low, 0.0)))
        product = jnp.dot(parts.astype(jnp.bfloat16), across[...], preferred_element_type=jnp.float32)
        scale = jnp.where(first, 1.0, scale_of(raw))
        stage[...] = jnp.sum(product, axis=0, keepdims=True) * scale

        @pl.when(jnp.logical_not(last))
        def _():
            chain(col + 1).start()

        for t in others:
            spread(t).start()
        weighted = stage[...]
        env_ref[...] = weighted * scale_of(weighted)

    for s in steps:
        out(s).wait_recv()
    out_ref[...] = oall[...]

    @pl.when(owner)
    def _():
        for t in others:
            spread(t).wait_send()

        @pl.when(jnp.logical_not(last))
        def _():
            chain(col + 1).wait_send()

    @pl.when(jnp.logical_not(owner))
    def _():
        spread(OWNER).wait_recv()
        weighted = landed[...]
        env_ref[...] = weighted * scale_of(weighted)
        gather(place.tile).wait_send()

    for s in steps:
        q1(s).wait_send()
        l2(s).wait_send()
        out(s).wait_send()
        for j in range(SIDE):
            q2(s, j).wait_send()

    @pl.when(first)
    def _():
        for s in steps:
            edge1(s).wait_send()

    @pl.when(jnp.logical_not(last))
    def _():
        for s in range(SIDE):
            l1(q_ref, s, col + 1).wait_send()


def new_site_of(basis, edge, whole_site, kron, closing, left_edge, cols, tiles):
    legs, share, width = basis.shape
    wide = width // SIDE
    bf16, f32 = jnp.bfloat16, jnp.float32
    dma = pltpu.SemaphoreType.DMA
    return pl.pallas_call(
        functools.partial(site_kernel, cols, tiles),
        out_shape=(
            jax.ShapeDtypeStruct((legs * share, width), bf16),
            jax.ShapeDtypeStruct((1, width), f32),
        ),
        in_specs=[VMEM, VMEM, pl.BlockSpec(memory_space=pl.ANY), VMEM, pl.BlockSpec(memory_space=pltpu.SMEM), VMEM],
        out_specs=(VMEM, VMEM),
        scratch_shapes=[
            pltpu.VMEM((legs, width, width), bf16),
            pltpu.VMEM((legs, width, wide), bf16),
            pltpu.VMEM((legs, width, wide), bf16),
            pltpu.VMEM((legs * wide, width), bf16),
            pltpu.VMEM((legs * wide, legs * wide), f32),
            pltpu.VMEM((legs, legs * wide, wide), bf16),
            pltpu.VMEM((legs, legs * wide, wide), bf16),
            pltpu.VMEM((legs * wide, wide), f32),
            pltpu.VMEM((legs * wide, wide), bf16),
            pltpu.VMEM((legs * share, width), bf16),
            pltpu.VMEM((wide, wide), bf16),
            pltpu.VMEM((width, width), bf16),
            pltpu.VMEM((1, width), f32),
            pltpu.VMEM((1, width), f32),
            pltpu.VMEM((1, width), f32),
            dma, dma((tiles,)), dma, dma, dma((tiles,)), dma,
            dma, dma,
            dma((SIDE - 1,)), dma((SIDE - 1,)),
            dma((SIDE - 1, SIDE)), dma((SIDE - 1, SIDE)),
            dma((SIDE,)), dma((SIDE,)),
            dma((2 * SIDE - 2,)), dma((SIDE - 1,)),
            dma((SIDE - 1,)), dma((SIDE - 1,)),
        ],
        compiler_params=pltpu.CompilerParams(collective_id=2, has_side_effects=True, vmem_limit_bytes=56 << 20),
    )(basis, edge, whole_site, kron, closing, left_edge.reshape(1, width))


def local(boundary, row_tensors, sketch_bond, sketch_phys, edge_factor, closing, left_edge):
    cols, tiles = lax.axis_size("col"), lax.axis_size("tile")
    share, legs, width = boundary.shape[1:]
    row_tensor = row_tensors[0]
    phys_map = jnp.einsum(
        "lurd,ldk->urk", row_tensor.astype(jnp.float32), sketch_phys[0].astype(jnp.float32), precision=HIGHEST
    )
    basis, whole_site = front(
        boundary[0].transpose(1, 0, 2), sketch_bond[0], phys_map.reshape(legs * legs, width))
    kron = jnp.einsum("lurd,st->ldsurt", row_tensor.astype(jnp.float32), jnp.eye(16, dtype=jnp.float32),
                      precision=HIGHEST)
    kron = kron.reshape(16 * legs * legs, 16 * legs * legs).astype(jnp.bfloat16)
    rows, env = new_site_of(
        basis, edge_factor.transpose(1, 0, 2), whole_site, kron, closing, left_edge, cols, tiles)
    new_site = rows.reshape(share // 16, legs, 16, width).transpose(0, 2, 1, 3).reshape(share, legs, width)
    env_local = lax.dynamic_slice(env, (0, lax.axis_index("tile") * share), (1, share))
    return (new_site[None], env_local)


def solution(mesh):
    in_specs = (
        P("col", "tile", None, None),
        P("col", None, None, None, None),
        P("col", "tile", None),
        P("col", None, None, None),
        P("tile", None, None),
        P("col", None),
        P(),
    )
    out_specs = (P("col", "tile", None, None), P("col", "tile"))
    return jax.shard_map(local, mesh=mesh, in_specs=in_specs, out_specs=out_specs, check_vma=False)
```

```python
import functools

import jax
import jax.numpy as jnp
from jax import lax
from jax.experimental import pallas as pl
from jax.experimental.pallas import tpu as pltpu
from jax.sharding import PartitionSpec as P

GRAM_SHIFT = 0.001
NB = 128
OWNER = 0
SIDE = 4
HIGHEST = lax.Precision.HIGHEST
MESH = pl.DeviceIdType.MESH
VMEM = pl.BlockSpec(memory_space=pltpu.VMEM)


def f32_dot(x, y, dims=(((1,), (0,)), ((), ()))):
    return lax.dot_general(x, y, dims, precision=HIGHEST, preferred_element_type=jnp.float32)


def factor_block(block, inv_ref):
    sub = lax.broadcasted_iota(jnp.int32, (8, NB), 0)
    lane = lax.broadcasted_iota(jnp.int32, (8, NB), 1)
    a0 = tuple(block[8 * i:8 * i + 8, :] for i in range(16))
    m0 = tuple((lane == sub + 8 * i).astype(jnp.float32) for i in range(16))

    def along(x, t):
        return jnp.broadcast_to(x[:, t:t + 1], (8, NB))

    def down(x, t):
        return jnp.broadcast_to(x[t:t + 1, :], (8, NB))

    def tree(terms):
        while len(terms) > 1:
            terms = [terms[i] + terms[i + 1] for i in range(0, len(terms), 2)]
        return terms[0]

    def group(count, g, carry):
        a, m, c = list(carry[0]), list(carry[1]), list(carry[2])
        p, n = a[0], m[0]
        done = jnp.zeros((8, NB), jnp.float32)
        for s in range(8):
            here = sub == s
            pivot = down(c[s], s)
            inv = 1.0 / pivot
            nrow = down(n, s)
            done = jnp.where(here, nrow * lax.rsqrt(pivot), done)
            column = c[s]

            def step(x, row):
                row = row * inv
                return jnp.where(here, row, x - column * row)

            for t in range(s + 1, 8):
                c[t] = step(c[t], down(c[t], s))
            p = step(p, down(p, s))
            n = step(n, nrow)
        inv_ref[pl.ds(pl.multiple_of(g * 8, 8), 8), :] = done
        prow = [down(p, t) for t in range(8)]
        nrow = [down(n, t) for t in range(8)]
        for i in range(1, count):
            x = [along(a[i], t) for t in range(8)]
            a[i] = a[i] - tree([x[t] * prow[t] for t in range(8)])
            m[i] = m[i] - tree([x[t] * nrow[t] for t in range(8)])
            if i == 1:
                c = [along(a[1], 8 + t) for t in range(8)]
        zero = jnp.zeros((8, NB), jnp.float32)
        return tuple(pltpu.roll(x, NB - 8, 1) for x in a[1:]) + (zero,), tuple(m[1:]) + (zero,), tuple(c)

    carry = (a0, m0, tuple(along(a0[0], t) for t in range(8)))
    for lo in range(0, 16, 4):
        carry = (carry[0][:16 - lo], carry[1][:16 - lo], carry[2])
        carry = lax.fori_loop(lo, lo + 4, functools.partial(group, 16 - lo), carry)


class Place:
    def __init__(self):
        tile = lax.axis_index("tile")
        self.tile = tile
        self.y, self.x = tile // SIDE, tile % SIDE

    def coordinate(self, axis):
        return self.x if axis == 0 else self.y

    def along(self, axis, index):
        return self.y * SIDE + index if axis == 0 else index * SIDE + self.x


def remote(src, dst, send, recv, where):
    return pltpu.make_async_remote_copy(
        src_ref=src, dst_ref=dst, send_sem=send, recv_sem=recv, device_id=where, device_id_type=MESH)


class LineGather:
    def __init__(self, place, axis, own, slot, sems, row=None):
        self.place, self.axis, self.own, self.slot, self.row = place, axis, own, slot, row
        self.send1, self.recv1, self.send2, self.recv2 = sems

    def first(self, s):
        place = self.place
        target = place.along(self.axis, (place.coordinate(self.axis) + s) % SIDE)
        return remote(self.own, self.slot(place.tile), self.send1.at[s - 1], self.recv1.at[s - 1], {"tile": target})

    def second(self, s, j):
        place = self.place
        other = 1 - self.axis
        target = place.along(other, (place.coordinate(other) + s) % SIDE)
        source = place.along(self.axis, (place.coordinate(self.axis) + SIDE - j) % SIDE)
        piece = self.own if j == 0 else self.slot(source)
        return remote(piece, self.slot(source), self.send2.at[s - 1, j], self.recv2.at[s - 1, j], {"tile": target})

    def start(self):
        for s in range(1, SIDE):
            self.first(s).start()

    def forward(self):
        for s in range(1, SIDE):
            self.second(s, 0).start()
        for j in range(1, SIDE):
            self.first(j).wait_recv()
            for s in range(1, SIDE):
                self.second(s, j).start()

    def finish(self):
        for s in range(1, SIDE):
            for j in range(SIDE):
                self.second(s, j).wait_recv()
        for s in range(1, SIDE):
            self.first(s).wait_send()
            for j in range(SIDE):
                self.second(s, j).wait_send()


LINE_SEMS = [
    pltpu.SemaphoreType.DMA((2, SIDE - 1)),
    pltpu.SemaphoreType.DMA((2, SIDE - 1)),
    pltpu.SemaphoreType.DMA((2, SIDE - 1, SIDE)),
    pltpu.SemaphoreType.DMA((2, SIDE - 1, SIDE)),
]


def kernel(cols, tiles, b_ref, g_ref, amat_ref, h_ref, edge_ref, close_ref, first_ref, out_ref, env_ref, *scratch):
    (gall, r_ref, part, total, s_ref, inv_ref, kron_ref, phys_ref, q_ref, ball, qall, lall, qt, x1, yh, yl, acc, osend, oall,
     tsend, across, arrived, stage, landed) = scratch[:24]
    land, middle, land2, own = scratch[24:26], scratch[26:28], scratch[28:30], scratch[30:32]
    g_sems, b_sems = scratch[32:36], scratch[36:40]
    rs1_send, rs1_recv, rs2_send, rs2_recv, ag1_send, ag1_recv, ag2_send, ag2_recv, here_sem = scratch[40:49]
    (gather_send, gather_recv, chain_send, chain_recv, spread_send, spread_recv, keep_sem, q1_send, q1_recv, q2_send, q2_recv,
     l1_send, l1_recv, l2_send, l2_recv, o_send, o_recv) = scratch[49:]
    place = Place()
    col = lax.axis_index("col")
    legs, share, width = b_ref.shape
    wide = width // SIDE
    first, last = col == 0, col == cols - 1
    barrier = pltpu.get_barrier_semaphore()

    def greet(where):
        pl.semaphore_signal(barrier, inc=1, device_id=where, device_id_type=MESH)

    for s in range(1, tiles):
        greet({"tile": (place.tile + s) % tiles})
    for i in range(SIDE):
        greet({"col": (col + cols - 1) % cols, "tile": place.along(0, i)})
    pl.semaphore_wait(barrier, tiles - 1 + SIDE)

    half = share // 2
    sketch = [
        LineGather(
            place, h, g_ref.at[h * half:h * half + half],
            lambda tile, h=h: gall.at[pl.ds(pl.multiple_of(tile * share + h * half, half), half)],
            [x.at[h] for x in g_sems])
        for h in (0, 1)
    ]
    for gather in sketch:
        gather.start()
    mine = pl.multiple_of(place.tile * share, share)
    gall[pl.ds(mine, share), :] = g_ref[...]
    keep = pltpu.make_async_copy(b_ref, ball.at[:, pl.ds(mine, share), :], here_sem)
    keep.start()
    legs_sq = legs * legs
    spread_rows = lax.broadcasted_iota(jnp.int32, (16 * legs_sq, legs_sq), 0) // 16
    spread_cols = lax.broadcasted_iota(jnp.int32, (16 * legs_sq, legs_sq), 1)
    repeat = (spread_rows == spread_cols).astype(jnp.float32)
    mixed = f32_dot(f32_dot(repeat, amat_ref[...].T), repeat, (((1,), (1,)), ((), ())))
    same = (lax.broadcasted_iota(jnp.int32, mixed.shape, 0) % 16) == (lax.broadcasted_iota(jnp.int32, mixed.shape, 1) % 16)
    kron_ref[...] = jnp.where(same, mixed, 0.0).astype(jnp.bfloat16)
    phys_ref[...] = f32_dot(
        amat_ref[...], jnp.concatenate([h_ref[l].astype(jnp.float32) for l in range(legs)], axis=0))
    for gather in sketch:
        gather.forward()
    for gather in sketch:
        gather.finish()

    def chunk(ref, index):
        return ref.at[:, :, pl.ds(pl.multiple_of(index * wide, wide), wide)]

    def slot(ref, tile, count=1):
        return ref.at[:, pl.ds(pl.multiple_of(tile * share, share), count * share), :]

    def q1(s):
        target = (place.y + s) % SIDE
        return remote(chunk(q_ref, target), slot(qall, place.tile), q1_send.at[s - 1], q1_recv.at[s - 1],
                      {"tile": place.along(1, target)})

    def q2(s, j):
        source = place.along(1, (place.y + SIDE - j) % SIDE)
        piece = chunk(q_ref, place.y) if j == 0 else slot(qall, source)
        return remote(piece, slot(qall, source), q2_send.at[s - 1, j], q2_recv.at[s - 1, j],
                      {"tile": place.along(0, (place.x + s) % SIDE)})

    def l1(ref, s, column):
        target = (place.x + s) % SIDE
        return remote(chunk(ref, target), slot(lall, place.tile), l1_send.at[s], l1_recv.at[s],
                      {"col": column, "tile": place.along(0, target)})

    def edge1(s):
        target = (place.x + s) % SIDE
        return remote(chunk(edge_ref, target), slot(lall, place.tile), l2_send.at[SIDE - 2 + s], l1_recv.at[s],
                      {"tile": place.along(0, target)})

    def l2(s):
        rows = slot(lall, place.y * SIDE, SIDE)
        return remote(rows, rows, l2_send.at[s - 1], l2_recv.at[s - 1],
                      {"tile": place.along(1, (place.y + s) % SIDE)})

    def edge_own():
        return pltpu.make_async_copy(chunk(edge_ref, place.x), slot(lall, place.tile), l1_recv.at[0])

    def send_chunk(index):
        step = (index - place.y + SIDE) % SIDE

        @pl.when(step > 0)
        def _():
            q1(step).start()

        @pl.when(jnp.logical_not(last))
        def _():
            l1(q_ref, (index - place.x + SIDE) % SIDE, col + 1).start()

    @pl.when(first)
    def _():
        edge_own().start()
        for s in range(1, SIDE):
            edge1(s).start()

    two = legs // 2
    sites = [
        LineGather(
            place, h, b_ref.at[h * two:h * two + two],
            lambda tile, h=h: ball.at[h * two:h * two + two, pl.ds(pl.multiple_of(tile * share, share), share), :],
            [x.at[h] for x in b_sems])
        for h in (0, 1)
    ]
    for gather in sites:
        gather.start()

    for u in range(legs):
        sketched = lax.dot_general(
            b_ref[u], gall[...], (((1,), (1,)), ((), ())), preferred_element_type=jnp.float32)
        for r in range(legs):
            term = sketched * phys_ref[u * legs + r:u * legs + r + 1, :]
            rows = slice(r * share, r * share + share)
            r_ref[rows, :] = term if u == 0 else r_ref[rows, :] + term

    blocks = width // NB
    pairs = blocks // 2
    packed = NB * (blocks + 1)
    cut = NB * (pairs + 1)
    columns = ((0, cut), (cut, packed))

    def view(ref, i):
        lo = 0 if i < pairs else (i + 1) * NB
        return ref.at[i if i < pairs else blocks - 1 - i, :, lo:lo + (blocks - i) * NB]

    flipped = r_ref[...].T
    for i in range(blocks):
        view(part, i)[...] = f32_dot(flipped[i * NB:i * NB + NB, :], r_ref[:, i * NB:])

    strip = NB // SIDE

    def line(h):
        axis = h
        c1, c2 = place.coordinate(axis), place.coordinate(1 - axis)
        lo, hi = columns[h]
        return axis, c1, c2, slice(lo, hi)

    def rs1(h, s):
        axis, c1, c2, cols = line(h)
        p = (c1 + s) % SIDE
        return remote(part.at[p, :, cols], land[h].at[s - 1], rs1_send.at[h, s - 1], rs1_recv.at[h, s - 1],
                      {"tile": place.along(axis, p)})

    def rs2(h, s):
        axis, c1, c2, cols = line(h)
        p = (c2 + s) % SIDE
        return remote(middle[h].at[pl.ds(pl.multiple_of(p * strip, strip), strip)], land2[h].at[s - 1],
                      rs2_send.at[h, s - 1], rs2_recv.at[h, s - 1], {"tile": place.along(1 - axis, p)})

    def ag1(h, s):
        axis, c1, c2, cols = line(h)
        p = (c2 + s) % SIDE
        return remote(own[h], total.at[c1, pl.ds(pl.multiple_of(c2 * strip, strip), strip), cols],
                      ag1_send.at[h, s - 1], ag1_recv.at[h, s - 1], {"tile": place.along(1 - axis, p)})

    def ag2(h, s):
        axis, c1, c2, cols = line(h)
        p = (c1 + s) % SIDE
        return remote(total.at[c1, :, cols], total.at[c1, :, cols], ag2_send.at[h, s - 1], ag2_recv.at[h, s - 1],
                      {"tile": place.along(axis, p)})

    steps = range(1, SIDE)
    for h in (0, 1):
        for s in steps:
            rs1(h, s).start()
    for h in (0, 1):
        axis, c1, c2, cols = line(h)
        for s in steps:
            rs1(h, s).wait_recv()
        middle[h][...] = ((part[c1, :, cols] + land[h][0]) + (land[h][1] + land[h][2]))
        for s in steps:
            rs2(h, s).start()
    for h in (0, 1):
        axis, c1, c2, cols = line(h)
        for s in steps:
            rs2(h, s).wait_recv()
        strip_rows = pl.ds(pl.multiple_of(c2 * strip, strip), strip)
        own[h][...] = ((middle[h][strip_rows, :] + land2[h][0]) + (land2[h][1] + land2[h][2]))
        for s in steps:
            ag1(h, s).start()
        total[c1, strip_rows, cols] = own[h][...]
    for h in (0, 1):
        for s in steps:
            ag1(h, s).wait_recv()
        for s in steps:
            ag2(h, s).start()
    for h in (0, 1):
        for s in steps:
            ag2(h, s).wait_recv()
    for h in (0, 1):
        for s in steps:
            for copy in (rs1, rs2, ag1, ag2):
                copy(h, s).wait_send()

    for gather in sites:
        gather.forward()

    eye = lax.broadcasted_iota(jnp.int32, (NB, NB), 0) == lax.broadcasted_iota(jnp.int32, (NB, NB), 1)
    for i in range(blocks):
        o, e = i * NB, i * NB + NB
        src = view(total, 0) if i == 0 else s_ref.at[o:e, o:]
        factor_block(src[:, :NB] + jnp.where(eye, GRAM_SHIFT, 0.0), inv_ref)
        inv = inv_ref[...]
        q = f32_dot(r_ref[:, o:e], inv, (((1,), (1,)), ((), ())))
        q_ref[:, :, o:e] = q.reshape(legs, share, NB).astype(q_ref.dtype)
        if e % wide == 0:
            send_chunk(e // wide - 1)
        if e == width:
            break
        upper = f32_dot(inv, src[:, NB:])
        r_ref[:, e:] = r_ref[:, e:] - f32_dot(q, upper)
        for k in range(i + 1, blocks):
            before = view(total, k)[...] if i == 0 else s_ref[k * NB:k * NB + NB, k * NB:]
            lo = (k - i - 1) * NB
            s_ref[k * NB:k * NB + NB, k * NB:] = before - f32_dot(upper[:, lo:lo + NB].T, upper[:, lo:])

    keep_q = pltpu.make_async_copy(chunk(q_ref, place.y), slot(qall, place.tile), keep_sem)
    keep_q.start()
    for s in steps:
        q2(s, 0).start()
    for j in steps:
        q1(j).wait_recv()
        for s in steps:
            q2(s, j).start()

    @pl.when(first)
    def _():
        edge_own().wait()
        for s in steps:
            edge1(s).wait_recv()

    @pl.when(jnp.logical_not(first))
    def _():
        for s in range(SIDE):
            l1(q_ref, s, col).wait_recv()

    for s in steps:
        l2(s).start()
    keep_q.wait()
    for s in steps:
        for j in range(SIDE):
            q2(s, j).wait_recv()
    for r in range(legs):
        qt[r * wide:r * wide + wide, :] = qall[r].astype(jnp.float32).T.astype(jnp.bfloat16)
    keep.wait()
    for gather in sites:
        gather.finish()

    groups = wide // 16
    acc[...] = jnp.zeros_like(acc)

    @pl.loop(0, width // wide)
    def _(piece):
        lanes = pl.ds(pl.multiple_of(piece * wide, wide), wide)
        for u in range(legs):
            x1[:, u * wide:u * wide + wide] = jnp.dot(
                qt[...], ball[u, :, lanes], preferred_element_type=jnp.float32)

        @pl.loop(0, groups // 2)
        def _(pair):
            for g in (pair * 2, pair * 2 + 1):
                start = pl.multiple_of(g * 16, 16)
                stack = jnp.concatenate(
                    [x1[pl.ds(pl.multiple_of(r * wide + start, 16), 16), u * wide:u * wide + wide]
                     for u in range(legs) for r in range(legs)], axis=0)
                high = stack.astype(jnp.bfloat16)
                low = (stack - high.astype(jnp.float32)).astype(jnp.bfloat16)
                y = (jnp.dot(kron_ref[...], high, preferred_element_type=jnp.float32)
                     + jnp.dot(kron_ref[...], low, preferred_element_type=jnp.float32))
                high = y.astype(jnp.bfloat16)
                low = (y - high.astype(jnp.float32)).astype(jnp.bfloat16)
                rows = pl.ds(pl.multiple_of(g * 64, 64), 64)
                for l in range(legs):
                    yh[l, rows, :] = high[l * 64:l * 64 + 64]
                    yl[l, rows, :] = low[l * 64:l * 64 + 64]

        @pl.when(piece == 0)
        def _():
            for s in steps:
                l2(s).wait_recv()

        for l in range(legs):
            left = lall[l, lanes, :]
            term = (jnp.dot(yh[l], left, preferred_element_type=jnp.float32)
                    + jnp.dot(yl[l], left, preferred_element_type=jnp.float32))
            acc[...] = acc[...] + term

    def out(s):
        target = (place.x + s) % SIDE
        return remote(osend.at[pl.ds(pl.multiple_of(target * wide, wide), wide)],
                      oall.at[:, pl.ds(pl.multiple_of(place.x * wide, wide), wide)],
                      o_send.at[s - 1], o_recv.at[s - 1], {"tile": place.along(0, target)})

    owner = place.tile == OWNER
    others = [t for t in range(tiles) if t != OWNER]
    block = (pl.ds(pl.multiple_of(place.x * wide, wide), wide), pl.ds(pl.multiple_of(place.y * wide, wide), wide))

    def gather(slot):
        return remote(tsend, across.at[block], gather_send, gather_recv.at[slot], {"tile": OWNER})

    def spread(where):
        return remote(stage, landed, spread_send.at[where], spread_recv, {"tile": where})

    def chain(where):
        return remote(stage, arrived, chain_send, chain_recv, {"col": where})

    def scale_of(raw):
        squares = jnp.sum(raw * raw, axis=1, keepdims=True)
        return jnp.sqrt(jnp.float32(width)) / jnp.sqrt(squares + 1e-06)

    osend[...] = acc[...].astype(jnp.bfloat16)
    rows = []
    for g in range(groups):
        t = None
        for d in range(legs):
            lo = (g * legs + d) * 16
            term = osend[lo:lo + 16, :].astype(jnp.float32) * close_ref[0, d]
            t = term if t is None else t + term
        rows.append(t)
    transfer = jnp.concatenate(rows, axis=0).astype(jnp.bfloat16).astype(jnp.float32)
    tsend[...] = transfer.T.astype(jnp.bfloat16)

    @pl.when(jnp.logical_not(owner))
    def _():
        gather(place.tile).start()

    for s in steps:
        out(s).start()
    mine = pl.multiple_of(place.x * wide, wide)
    oall[:, pl.ds(mine, wide)] = osend[pl.ds(mine, wide), :]

    @pl.when(owner)
    def _():
        across[block] = tsend[...]
        for t in others:
            gather(t).wait_recv()

        @pl.when(first)
        def _():
            arrived[...] = first_ref[...]

        @pl.when(jnp.logical_not(first))
        def _():
            chain(col).wait_recv()

        raw = arrived[...]
        high = raw.astype(jnp.bfloat16).astype(jnp.float32)
        middle = (raw - high).astype(jnp.bfloat16).astype(jnp.float32)
        low = raw - high - middle
        row = lax.broadcasted_iota(jnp.int32, (8, width), 0)
        parts = jnp.where(row == 0, high, jnp.where(row == 1, middle, jnp.where(row == 2, low, 0.0)))
        product = jnp.dot(parts.astype(jnp.bfloat16), across[...], preferred_element_type=jnp.float32)
        scale = jnp.where(first, 1.0, scale_of(raw))
        stage[...] = jnp.sum(product, axis=0, keepdims=True) * scale

        @pl.when(jnp.logical_not(last))
        def _():
            chain(col + 1).start()

        for t in others:
            spread(t).start()
        weighted = stage[...]
        env_ref[...] = weighted * scale_of(weighted)

    for s in steps:
        out(s).wait_recv()
    out_ref[...] = oall[...]

    @pl.when(owner)
    def _():
        for t in others:
            spread(t).wait_send()

        @pl.when(jnp.logical_not(last))
        def _():
            chain(col + 1).wait_send()

    @pl.when(jnp.logical_not(owner))
    def _():
        spread(OWNER).wait_recv()
        weighted = landed[...]
        env_ref[...] = weighted * scale_of(weighted)
        gather(place.tile).wait_send()

    for s in steps:
        q1(s).wait_send()
        l2(s).wait_send()
        out(s).wait_send()
        for j in range(SIDE):
            q2(s, j).wait_send()

    @pl.when(first)
    def _():
        for s in steps:
            edge1(s).wait_send()

    @pl.when(jnp.logical_not(last))
    def _():
        for s in range(SIDE):
            l1(q_ref, s, col + 1).wait_send()


def absorb(site, sketch, amat, phys, edge, closing, left_edge, cols, tiles):
    legs, share, width = site.shape
    wide = width // SIDE
    packed = width + NB
    cut = NB * (width // NB // 2 + 1)
    sizes = (cut, packed - cut)
    strip = NB // SIDE
    bf16, f32 = jnp.bfloat16, jnp.float32
    dma = pltpu.SemaphoreType.DMA
    three = dma((2, SIDE - 1))
    vmem = pltpu.VMEM
    return pl.pallas_call(
        functools.partial(kernel, cols, tiles),
        out_shape=(
            jax.ShapeDtypeStruct((legs * share, width), bf16),
            jax.ShapeDtypeStruct((1, width), f32),
        ),
        in_specs=[VMEM] * 5 + [pl.BlockSpec(memory_space=pltpu.SMEM), VMEM],
        out_specs=(VMEM, VMEM),
        scratch_shapes=[
            vmem((width, width), bf16),
            vmem((legs * share, width), f32),
            vmem((SIDE, NB, packed), f32),
            vmem((SIDE, NB, packed), f32),
            vmem((width, width), f32),
            vmem((NB, NB), f32),
            vmem((16 * legs * legs, 16 * legs * legs), bf16),
            vmem((legs * legs, width), f32),
            vmem((legs, share, width), bf16),
            vmem((legs, width, width), bf16),
            vmem((legs, width, wide), bf16),
            vmem((legs, width, wide), bf16),
            vmem((legs * wide, width), bf16),
            vmem((legs * wide, legs * wide), f32),
            vmem((legs, legs * wide, wide), bf16),
            vmem((legs, legs * wide, wide), bf16),
            vmem((legs * wide, wide), f32),
            vmem((legs * wide, wide), bf16),
            vmem((legs * share, width), bf16),
            vmem((wide, wide), bf16),
            vmem((width, width), bf16),
            vmem((1, width), f32),
            vmem((1, width), f32),
            vmem((1, width), f32),
            *[vmem((SIDE - 1, NB, size), f32) for size in sizes],
            *[vmem((NB, size), f32) for size in sizes],
            *[vmem((SIDE - 1, strip, size), f32) for size in sizes],
            *[vmem((strip, size), f32) for size in sizes],
            *LINE_SEMS,
            *LINE_SEMS,
            *[three] * 8,
            dma,
            dma, dma((tiles,)), dma, dma, dma((tiles,)), dma,
            dma,
            dma((SIDE - 1,)), dma((SIDE - 1,)),
            dma((SIDE - 1, SIDE)), dma((SIDE - 1, SIDE)),
            dma((SIDE,)), dma((SIDE,)),
            dma((2 * SIDE - 2,)), dma((SIDE - 1,)),
            dma((SIDE - 1,)), dma((SIDE - 1,)),
        ],
        compiler_params=pltpu.CompilerParams(collective_id=0, has_side_effects=True, vmem_limit_bytes=62 << 20),
    )(site, sketch, amat, phys, edge, closing, left_edge.reshape(1, width))


def local(boundary, row_tensors, sketch_bond, sketch_phys, edge_factor, closing, left_edge):
    cols, tiles = lax.axis_size("col"), lax.axis_size("tile")
    share, legs, width = boundary.shape[1:]
    amat = row_tensors[0].astype(jnp.float32).transpose(1, 2, 0, 3).reshape(legs * legs, legs * legs)
    rows, env = absorb(
        boundary[0].transpose(1, 0, 2), sketch_bond[0], amat, sketch_phys[0], edge_factor.transpose(1, 0, 2),
        closing, left_edge, cols, tiles)
    new_site = rows.reshape(share // 16, legs, 16, width).transpose(0, 2, 1, 3).reshape(share, legs, width)
    env_local = lax.dynamic_slice(env, (0, lax.axis_index("tile") * share), (1, share))
    return (new_site[None], env_local)


def solution(mesh):
    in_specs = (
        P("col", "tile", None, None),
        P("col", None, None, None, None),
        P("col", "tile", None),
        P("col", None, None, None),
        P("tile", None, None),
        P("col", None),
        P(),
    )
    out_specs = (P("col", "tile", None, None), P("col", "tile"))
    return jax.shard_map(local, mesh=mesh, in_specs=in_specs, out_specs=out_specs, check_vma=False)
```

```python
import functools

import jax
import jax.numpy as jnp
from jax import lax
from jax.experimental import pallas as pl
from jax.experimental.pallas import tpu as pltpu
from jax.sharding import PartitionSpec as P

GRAM_SHIFT = 0.001
NB = 128
OWNER = 0
SIDE = 4
HIGHEST = lax.Precision.HIGHEST
MESH = pl.DeviceIdType.MESH
VMEM = pl.BlockSpec(memory_space=pltpu.VMEM)


def f32_dot(x, y, dims=(((1,), (0,)), ((), ()))):
    return lax.dot_general(x, y, dims, precision=HIGHEST, preferred_element_type=jnp.float32)


def factor_block(block, inv_ref):
    sub = lax.broadcasted_iota(jnp.int32, (8, NB), 0)
    lane = lax.broadcasted_iota(jnp.int32, (8, NB), 1)
    a0 = tuple(block[8 * i:8 * i + 8, :] for i in range(16))
    m0 = tuple((lane == sub + 8 * i).astype(jnp.float32) for i in range(16))

    def along(x, t):
        return jnp.broadcast_to(x[:, t:t + 1], (8, NB))

    def down(x, t):
        return jnp.broadcast_to(x[t:t + 1, :], (8, NB))

    def tree(terms):
        while len(terms) > 1:
            terms = [terms[i] + terms[i + 1] for i in range(0, len(terms), 2)]
        return terms[0]

    def group(count, g, carry):
        a, m, c = list(carry[0]), list(carry[1]), list(carry[2])
        p, n = a[0], m[0]
        done = jnp.zeros((8, NB), jnp.float32)
        for s in range(8):
            here = sub == s
            pivot = down(c[s], s)
            inv = 1.0 / pivot
            nrow = down(n, s)
            done = jnp.where(here, nrow * lax.rsqrt(pivot), done)
            column = c[s]

            def step(x, row):
                row = row * inv
                return jnp.where(here, row, x - column * row)

            for t in range(s + 1, 8):
                c[t] = step(c[t], down(c[t], s))
            p = step(p, down(p, s))
            n = step(n, nrow)
        inv_ref[pl.ds(pl.multiple_of(g * 8, 8), 8), :] = done
        prow = [down(p, t) for t in range(8)]
        nrow = [down(n, t) for t in range(8)]
        for i in range(1, count):
            x = [along(a[i], t) for t in range(8)]
            a[i] = a[i] - tree([x[t] * prow[t] for t in range(8)])
            m[i] = m[i] - tree([x[t] * nrow[t] for t in range(8)])
            if i == 1:
                c = [along(a[1], 8 + t) for t in range(8)]
        zero = jnp.zeros((8, NB), jnp.float32)
        return tuple(pltpu.roll(x, NB - 8, 1) for x in a[1:]) + (zero,), tuple(m[1:]) + (zero,), tuple(c)

    carry = (a0, m0, tuple(along(a0[0], t) for t in range(8)))
    for lo in range(0, 16, 4):
        carry = (carry[0][:16 - lo], carry[1][:16 - lo], carry[2])
        carry = lax.fori_loop(lo, lo + 4, functools.partial(group, 16 - lo), carry)


class Place:
    def __init__(self):
        tile = lax.axis_index("tile")
        self.tile = tile
        self.y, self.x = tile // SIDE, tile % SIDE

    def coordinate(self, axis):
        return self.x if axis == 0 else self.y

    def along(self, axis, index):
        return self.y * SIDE + index if axis == 0 else index * SIDE + self.x


def remote(src, dst, send, recv, where):
    return pltpu.make_async_remote_copy(
        src_ref=src, dst_ref=dst, send_sem=send, recv_sem=recv, device_id=where, device_id_type=MESH)


class LineGather:
    def __init__(self, place, axis, own, slot, sems, row=None):
        self.place, self.axis, self.own, self.slot, self.row = place, axis, own, slot, row
        self.send1, self.recv1, self.send2, self.recv2 = sems

    def first(self, s):
        place = self.place
        target = place.along(self.axis, (place.coordinate(self.axis) + s) % SIDE)
        return remote(self.own, self.slot(place.tile), self.send1.at[s - 1], self.recv1.at[s - 1], {"tile": target})

    def second(self, s, j):
        place = self.place
        other = 1 - self.axis
        target = place.along(other, (place.coordinate(other) + s) % SIDE)
        source = place.along(self.axis, (place.coordinate(self.axis) + SIDE - j) % SIDE)
        piece = self.own if j == 0 else self.slot(source)
        return remote(piece, self.slot(source), self.send2.at[s - 1, j], self.recv2.at[s - 1, j], {"tile": target})

    def start(self):
        for s in range(1, SIDE):
            self.first(s).start()

    def forward(self):
        for s in range(1, SIDE):
            self.second(s, 0).start()
        for j in range(1, SIDE):
            self.first(j).wait_recv()
            for s in range(1, SIDE):
                self.second(s, j).start()

    def finish(self):
        for s in range(1, SIDE):
            for j in range(SIDE):
                self.second(s, j).wait_recv()
        for s in range(1, SIDE):
            self.first(s).wait_send()
            for j in range(SIDE):
                self.second(s, j).wait_send()


LINE_SEMS = [
    pltpu.SemaphoreType.DMA((2, SIDE - 1)),
    pltpu.SemaphoreType.DMA((2, SIDE - 1)),
    pltpu.SemaphoreType.DMA((2, SIDE - 1, SIDE)),
    pltpu.SemaphoreType.DMA((2, SIDE - 1, SIDE)),
]


def kernel(cols, tiles, b_ref, g_ref, amat_ref, h_ref, edge_ref, close_ref, first_ref, out_ref, env_ref, *scratch):
    (gall, r_ref, part, total, s_ref, inv_ref, kron_ref, phys_ref, q_ref, ball, qall, lall, qt, x1, yh, yl, acc, osend, oall,
     tsend, across, arrived, stage, landed) = scratch[:24]
    land, middle, land2, own = scratch[24:26], scratch[26:28], scratch[28:30], scratch[30:32]
    g_sems, b_sems = scratch[32:36], scratch[36:40]
    rs1_send, rs1_recv, rs2_send, rs2_recv, ag1_send, ag1_recv, ag2_send, ag2_recv, here_sem = scratch[40:49]
    (gather_send, gather_recv, chain_send, chain_recv, spread_send, spread_recv, keep_sem, q1_send, q1_recv, q2_send, q2_recv,
     l1_send, l1_recv, l2_send, l2_recv, o_send, o_recv) = scratch[49:]
    place = Place()
    col = lax.axis_index("col")
    legs, share, width = b_ref.shape
    wide = width // SIDE
    first, last = col == 0, col == cols - 1
    barrier = pltpu.get_barrier_semaphore()

    def greet(where):
        pl.semaphore_signal(barrier, inc=1, device_id=where, device_id_type=MESH)

    for s in range(1, tiles):
        greet({"tile": (place.tile + s) % tiles})
    for i in range(SIDE):
        greet({"col": (col + cols - 1) % cols, "tile": place.along(0, i)})
    pl.semaphore_wait(barrier, tiles - 1 + SIDE)

    half = share // 2
    sketch = [
        LineGather(
            place, h, g_ref.at[h * half:h * half + half],
            lambda tile, h=h: gall.at[pl.ds(pl.multiple_of(tile * share + h * half, half), half)],
            [x.at[h] for x in g_sems])
        for h in (0, 1)
    ]
    for gather in sketch:
        gather.start()
    mine = pl.multiple_of(place.tile * share, share)
    gall[pl.ds(mine, share), :] = g_ref[...]
    keep = pltpu.make_async_copy(b_ref, ball.at[:, pl.ds(mine, share), :], here_sem)
    keep.start()
    legs_sq = legs * legs
    spread_rows = lax.broadcasted_iota(jnp.int32, (16 * legs_sq, legs_sq), 0) // 16
    spread_cols = lax.broadcasted_iota(jnp.int32, (16 * legs_sq, legs_sq), 1)
    repeat = (spread_rows == spread_cols).astype(jnp.float32)
    mixed = f32_dot(f32_dot(repeat, amat_ref[...].T), repeat, (((1,), (1,)), ((), ())))
    same = (lax.broadcasted_iota(jnp.int32, mixed.shape, 0) % 16) == (lax.broadcasted_iota(jnp.int32, mixed.shape, 1) % 16)
    kron_ref[...] = jnp.where(same, mixed, 0.0).astype(jnp.bfloat16)
    phys_ref[...] = f32_dot(
        amat_ref[...], jnp.concatenate([h_ref[l].astype(jnp.float32) for l in range(legs)], axis=0))
    for gather in sketch:
        gather.forward()
    for gather in sketch:
        gather.finish()

    def chunk(ref, index):
        return ref.at[:, :, pl.ds(pl.multiple_of(index * wide, wide), wide)]

    def slot(ref, tile, count=1):
        return ref.at[:, pl.ds(pl.multiple_of(tile * share, share), count * share), :]

    def q1(s):
        target = (place.y + s) % SIDE
        return remote(chunk(q_ref, target), slot(qall, place.tile), q1_send.at[s - 1], q1_recv.at[s - 1],
                      {"tile": place.along(1, target)})

    def q2(s, j):
        source = place.along(1, (place.y + SIDE - j) % SIDE)
        piece = chunk(q_ref, place.y) if j == 0 else slot(qall, source)
        return remote(piece, slot(qall, source), q2_send.at[s - 1, j], q2_recv.at[s - 1, j],
                      {"tile": place.along(0, (place.x + s) % SIDE)})

    def l1(ref, s, column):
        target = (place.x + s) % SIDE
        return remote(chunk(ref, target), slot(lall, place.tile), l1_send.at[s], l1_recv.at[s],
                      {"col": column, "tile": place.along(0, target)})

    def edge1(s):
        target = (place.x + s) % SIDE
        return remote(chunk(edge_ref, target), slot(lall, place.tile), l2_send.at[SIDE - 2 + s], l1_recv.at[s],
                      {"tile": place.along(0, target)})

    def l2(s):
        rows = slot(lall, place.y * SIDE, SIDE)
        return remote(rows, rows, l2_send.at[s - 1], l2_recv.at[s - 1],
                      {"tile": place.along(1, (place.y + s) % SIDE)})

    def edge_own():
        return pltpu.make_async_copy(chunk(edge_ref, place.x), slot(lall, place.tile), l1_recv.at[0])

    def send_chunk(index):
        step = (index - place.y + SIDE) % SIDE

        @pl.when(step > 0)
        def _():
            q1(step).start()

        @pl.when(jnp.logical_not(last))
        def _():
            l1(q_ref, (index - place.x + SIDE) % SIDE, col + 1).start()

    @pl.when(first)
    def _():
        edge_own().start()
        for s in range(1, SIDE):
            edge1(s).start()

    two = legs // 2
    sites = [
        LineGather(
            place, h, b_ref.at[h * two:h * two + two],
            lambda tile, h=h: ball.at[h * two:h * two + two, pl.ds(pl.multiple_of(tile * share, share), share), :],
            [x.at[h] for x in b_sems])
        for h in (0, 1)
    ]
    for gather in sites:
        gather.start()

    for u in range(legs):
        sketched = lax.dot_general(
            b_ref[u], gall[...], (((1,), (1,)), ((), ())), preferred_element_type=jnp.float32)
        for r in range(legs):
            term = sketched * phys_ref[u * legs + r:u * legs + r + 1, :]
            rows = slice(r * share, r * share + share)
            r_ref[rows, :] = term if u == 0 else r_ref[rows, :] + term

    blocks = width // NB
    pairs = blocks // 2
    packed = NB * (blocks + 1)
    cut = NB * (pairs + 1)
    columns = ((0, cut), (cut, packed))

    def view(ref, i):
        lo = 0 if i < pairs else (i + 1) * NB
        return ref.at[i if i < pairs else blocks - 1 - i, :, lo:lo + (blocks - i) * NB]

    flipped = r_ref[...].T
    strip = NB // SIDE

    def line(h):
        axis = h
        c1, c2 = place.coordinate(axis), place.coordinate(1 - axis)
        lo, hi = columns[h]
        return axis, c1, c2, slice(lo, hi)

    def rs1(h, s):
        axis, c1, c2, cols = line(h)
        p = (c1 + s) % SIDE
        return remote(part.at[p, :, cols], land[h].at[s - 1], rs1_send.at[h, s - 1], rs1_recv.at[h, s - 1],
                      {"tile": place.along(axis, p)})

    def rs2(h, s):
        axis, c1, c2, cols = line(h)
        p = (c2 + s) % SIDE
        return remote(middle[h].at[pl.ds(pl.multiple_of(p * strip, strip), strip)], land2[h].at[s - 1],
                      rs2_send.at[h, s - 1], rs2_recv.at[h, s - 1], {"tile": place.along(1 - axis, p)})

    def ag1(h, s):
        axis, c1, c2, cols = line(h)
        p = (c2 + s) % SIDE
        return remote(own[h], total.at[c1, pl.ds(pl.multiple_of(c2 * strip, strip), strip), cols],
                      ag1_send.at[h, s - 1], ag1_recv.at[h, s - 1], {"tile": place.along(1 - axis, p)})

    def ag2(h, s):
        axis, c1, c2, cols = line(h)
        p = (c1 + s) % SIDE
        return remote(total.at[c1, :, cols], total.at[c1, :, cols], ag2_send.at[h, s - 1], ag2_recv.at[h, s - 1],
                      {"tile": place.along(axis, p)})

    steps = range(1, SIDE)

    def send_pair(h, pair):
        step = (pair - place.coordinate(h) + SIDE) % SIDE

        @pl.when(step > 0)
        def _():
            rs1(h, step).start()

    for pair in range(pairs):
        for i in (pair, blocks - 1 - pair):
            view(part, i)[...] = f32_dot(flipped[i * NB:i * NB + NB, :], r_ref[:, i * NB:])
        for h in (0, 1):
            send_pair(h, pair)
    for h in (0, 1):
        axis, c1, c2, cols = line(h)
        for s in steps:
            rs1(h, s).wait_recv()
        middle[h][...] = ((part[c1, :, cols] + land[h][0]) + (land[h][1] + land[h][2]))
        for s in steps:
            rs2(h, s).start()
    for h in (0, 1):
        axis, c1, c2, cols = line(h)
        for s in steps:
            rs2(h, s).wait_recv()
        strip_rows = pl.ds(pl.multiple_of(c2 * strip, strip), strip)
        own[h][...] = ((middle[h][strip_rows, :] + land2[h][0]) + (land2[h][1] + land2[h][2]))
        for s in steps:
            ag1(h, s).start()
        total[c1, strip_rows, cols] = own[h][...]
    for h in (0, 1):
        for s in steps:
            ag1(h, s).wait_recv()
        for s in steps:
            ag2(h, s).start()
    for h in (0, 1):
        for s in steps:
            ag2(h, s).wait_recv()
    for h in (0, 1):
        for s in steps:
            for copy in (rs1, rs2, ag1, ag2):
                copy(h, s).wait_send()

    for gather in sites:
        gather.forward()

    eye = lax.broadcasted_iota(jnp.int32, (NB, NB), 0) == lax.broadcasted_iota(jnp.int32, (NB, NB), 1)
    for i in range(blocks):
        o, e = i * NB, i * NB + NB
        src = view(total, 0) if i == 0 else s_ref.at[o:e, o:]
        factor_block(src[:, :NB] + jnp.where(eye, GRAM_SHIFT, 0.0), inv_ref)
        inv = inv_ref[...]
        q = f32_dot(r_ref[:, o:e], inv, (((1,), (1,)), ((), ())))
        q_ref[:, :, o:e] = q.reshape(legs, share, NB).astype(q_ref.dtype)
        if e % wide == 0:
            send_chunk(e // wide - 1)
        if e == width:
            break
        upper = f32_dot(inv, src[:, NB:])
        r_ref[:, e:] = r_ref[:, e:] - f32_dot(q, upper)
        for k in range(i + 1, blocks):
            before = view(total, k)[...] if i == 0 else s_ref[k * NB:k * NB + NB, k * NB:]
            lo = (k - i - 1) * NB
            s_ref[k * NB:k * NB + NB, k * NB:] = before - f32_dot(upper[:, lo:lo + NB].T, upper[:, lo:])

    keep_q = pltpu.make_async_copy(chunk(q_ref, place.y), slot(qall, place.tile), keep_sem)
    keep_q.start()
    for s in steps:
        q2(s, 0).start()
    for j in steps:
        q1(j).wait_recv()
        for s in steps:
            q2(s, j).start()

    @pl.when(first)
    def _():
        edge_own().wait()
        for s in steps:
            edge1(s).wait_recv()

    @pl.when(jnp.logical_not(first))
    def _():
        for s in range(SIDE):
            l1(q_ref, s, col).wait_recv()

    for s in steps:
        l2(s).start()
    keep_q.wait()
    for s in steps:
        for j in range(SIDE):
            q2(s, j).wait_recv()
    part_k = wide // 2
    for r in range(legs):
        turned = qall[r].astype(jnp.float32).T.astype(jnp.bfloat16)
        for h in (0, 1):
            lo = (h * legs + r) * part_k
            qt[lo:lo + part_k, :] = turned[h * part_k:h * part_k + part_k]
    keep.wait()
    for gather in sites:
        gather.finish()

    def out(s):
        target = (place.x + s) % SIDE
        return remote(osend.at[pl.ds(pl.multiple_of(target * wide, wide), wide)],
                      oall.at[:, pl.ds(pl.multiple_of(place.x * wide, wide), wide)],
                      o_send.at[s - 1], o_recv.at[s - 1], {"tile": place.along(0, target)})

    owner = place.tile == OWNER
    others = [t for t in range(tiles) if t != OWNER]

    def block(h):
        return (pl.ds(pl.multiple_of(place.x * wide, wide), wide),
                pl.ds(pl.multiple_of(place.y * wide + h * part_k, part_k), part_k))

    def gather(h, slot):
        return remote(tsend.at[h], across.at[block(h)], gather_send.at[h], gather_recv.at[h, slot], {"tile": OWNER})

    def spread(where):
        return remote(stage, landed, spread_send.at[where], spread_recv, {"tile": where})

    def chain(where):
        return remote(stage, arrived, chain_send, chain_recv, {"col": where})

    def scale_of(raw):
        squares = jnp.sum(raw * raw, axis=1, keepdims=True)
        return jnp.sqrt(jnp.float32(width)) / jnp.sqrt(squares + 1e-06)

    groups = part_k // 16
    unroll = 4
    for h in (0, 1):
        acc[...] = jnp.zeros_like(acc)
        base = h * legs * part_k

        @pl.loop(0, width // wide)
        def _(piece):
            lanes = pl.ds(pl.multiple_of(piece * wide, wide), wide)
            for u in range(legs):
                x1[:, u * wide:u * wide + wide] = jnp.dot(
                    qt[base:base + legs * part_k, :], ball[u, :, lanes], preferred_element_type=jnp.float32)

            @pl.loop(0, groups // unroll)
            def _(some):
                for g in [some * unroll + k for k in range(unroll)]:
                    start = pl.multiple_of(g * 16, 16)
                    stack = jnp.concatenate(
                        [x1[pl.ds(pl.multiple_of(r * part_k + start, 16), 16), u * wide:u * wide + wide]
                         for u in range(legs) for r in range(legs)], axis=0)
                    high = stack.astype(jnp.bfloat16)
                    low = (stack - high.astype(jnp.float32)).astype(jnp.bfloat16)
                    y = (jnp.dot(kron_ref[...], high, preferred_element_type=jnp.float32)
                         + jnp.dot(kron_ref[...], low, preferred_element_type=jnp.float32))
                    high = y.astype(jnp.bfloat16)
                    low = (y - high.astype(jnp.float32)).astype(jnp.bfloat16)
                    rows = pl.ds(pl.multiple_of(g * 64, 64), 64)
                    for l in range(legs):
                        yh[l, rows, :] = high[l * 64:l * 64 + 64]
                        yl[l, rows, :] = low[l * 64:l * 64 + 64]

            if h == 0:
                @pl.when(piece == 0)
                def _():
                    for s in steps:
                        l2(s).wait_recv()

            for l in range(legs):
                left = lall[l, lanes, :]
                term = (jnp.dot(yh[l], left, preferred_element_type=jnp.float32)
                        + jnp.dot(yl[l], left, preferred_element_type=jnp.float32))
                acc[...] = acc[...] + term

        osend[base:base + legs * part_k, :] = acc[...].astype(jnp.bfloat16)
        strips = []
        for g in range(groups):
            t = None
            for d in range(legs):
                lo = base + (g * legs + d) * 16
                term = osend[lo:lo + 16, :].astype(jnp.float32) * close_ref[0, d]
                t = term if t is None else t + term
            strips.append(t)
        transfer = jnp.concatenate(strips, axis=0).astype(jnp.bfloat16).astype(jnp.float32)
        tsend[h] = transfer.T.astype(jnp.bfloat16)

        @pl.when(jnp.logical_not(owner))
        def _():
            gather(h, place.tile).start()

    for s in steps:
        out(s).start()
    mine = pl.multiple_of(place.x * wide, wide)
    oall[:, pl.ds(mine, wide)] = osend[pl.ds(mine, wide), :]

    @pl.when(owner)
    def _():
        for h in (0, 1):
            across[block(h)] = tsend[h]
            for t in others:
                gather(h, t).wait_recv()

        @pl.when(first)
        def _():
            arrived[...] = first_ref[...]

        @pl.when(jnp.logical_not(first))
        def _():
            chain(col).wait_recv()

        raw = arrived[...]
        high = raw.astype(jnp.bfloat16).astype(jnp.float32)
        middle = (raw - high).astype(jnp.bfloat16).astype(jnp.float32)
        low = raw - high - middle
        row = lax.broadcasted_iota(jnp.int32, (8, width), 0)
        parts = jnp.where(row == 0, high, jnp.where(row == 1, middle, jnp.where(row == 2, low, 0.0)))
        product = jnp.dot(parts.astype(jnp.bfloat16), across[...], preferred_element_type=jnp.float32)
        scale = jnp.where(first, 1.0, scale_of(raw))
        stage[...] = jnp.sum(product, axis=0, keepdims=True) * scale

        @pl.when(jnp.logical_not(last))
        def _():
            chain(col + 1).start()

        for t in others:
            spread(t).start()
        weighted = stage[...]
        env_ref[...] = weighted * scale_of(weighted)

    for s in steps:
        out(s).wait_recv()
    out_ref[...] = oall[...]

    @pl.when(owner)
    def _():
        for t in others:
            spread(t).wait_send()

        @pl.when(jnp.logical_not(last))
        def _():
            chain(col + 1).wait_send()

    @pl.when(jnp.logical_not(owner))
    def _():
        spread(OWNER).wait_recv()
        weighted = landed[...]
        env_ref[...] = weighted * scale_of(weighted)
        for h in (0, 1):
            gather(h, place.tile).wait_send()

    for s in steps:
        q1(s).wait_send()
        l2(s).wait_send()
        out(s).wait_send()
        for j in range(SIDE):
            q2(s, j).wait_send()

    @pl.when(first)
    def _():
        for s in steps:
            edge1(s).wait_send()

    @pl.when(jnp.logical_not(last))
    def _():
        for s in range(SIDE):
            l1(q_ref, s, col + 1).wait_send()


def absorb(site, sketch, amat, phys, edge, closing, left_edge, cols, tiles):
    legs, share, width = site.shape
    wide = width // SIDE
    packed = width + NB
    cut = NB * (width // NB // 2 + 1)
    sizes = (cut, packed - cut)
    strip = NB // SIDE
    bf16, f32 = jnp.bfloat16, jnp.float32
    dma = pltpu.SemaphoreType.DMA
    three = dma((2, SIDE - 1))
    vmem = pltpu.VMEM
    return pl.pallas_call(
        functools.partial(kernel, cols, tiles),
        out_shape=(
            jax.ShapeDtypeStruct((legs * share, width), bf16),
            jax.ShapeDtypeStruct((1, width), f32),
        ),
        in_specs=[VMEM] * 5 + [pl.BlockSpec(memory_space=pltpu.SMEM), VMEM],
        out_specs=(VMEM, VMEM),
        scratch_shapes=[
            vmem((width, width), bf16),
            vmem((legs * share, width), f32),
            vmem((SIDE, NB, packed), f32),
            vmem((SIDE, NB, packed), f32),
            vmem((width, width), f32),
            vmem((NB, NB), f32),
            vmem((16 * legs * legs, 16 * legs * legs), bf16),
            vmem((legs * legs, width), f32),
            vmem((legs, share, width), bf16),
            vmem((legs, width, width), bf16),
            vmem((legs, width, wide), bf16),
            vmem((legs, width, wide), bf16),
            vmem((legs * wide, width), bf16),
            vmem((legs * wide // 2, legs * wide), f32),
            vmem((legs, legs * wide // 2, wide), bf16),
            vmem((legs, legs * wide // 2, wide), bf16),
            vmem((legs * wide // 2, wide), f32),
            vmem((legs * wide, wide), bf16),
            vmem((legs * share, width), bf16),
            vmem((2, wide, wide // 2), bf16),
            vmem((width, width), bf16),
            vmem((1, width), f32),
            vmem((1, width), f32),
            vmem((1, width), f32),
            *[vmem((SIDE - 1, NB, size), f32) for size in sizes],
            *[vmem((NB, size), f32) for size in sizes],
            *[vmem((SIDE - 1, strip, size), f32) for size in sizes],
            *[vmem((strip, size), f32) for size in sizes],
            *LINE_SEMS,
            *LINE_SEMS,
            *[three] * 8,
            dma,
            dma((2,)), dma((2, tiles)), dma, dma, dma((tiles,)), dma,
            dma,
            dma((SIDE - 1,)), dma((SIDE - 1,)),
            dma((SIDE - 1, SIDE)), dma((SIDE - 1, SIDE)),
            dma((SIDE,)), dma((SIDE,)),
            dma((2 * SIDE - 2,)), dma((SIDE - 1,)),
            dma((SIDE - 1,)), dma((SIDE - 1,)),
        ],
        compiler_params=pltpu.CompilerParams(collective_id=0, has_side_effects=True, vmem_limit_bytes=62 << 20),
    )(site, sketch, amat, phys, edge, closing, left_edge.reshape(1, width))


def local(boundary, row_tensors, sketch_bond, sketch_phys, edge_factor, closing, left_edge):
    cols, tiles = lax.axis_size("col"), lax.axis_size("tile")
    share, legs, width = boundary.shape[1:]
    amat = row_tensors[0].astype(jnp.float32).transpose(1, 2, 0, 3).reshape(legs * legs, legs * legs)
    rows, env = absorb(
        boundary[0].transpose(1, 0, 2), sketch_bond[0], amat, sketch_phys[0], edge_factor.transpose(1, 0, 2),
        closing, left_edge, cols, tiles)
    new_site = rows.reshape(share // 16, legs, 16, width).transpose(0, 2, 1, 3).reshape(share, legs, width)
    env_local = lax.dynamic_slice(env, (0, lax.axis_index("tile") * share), (1, share))
    return (new_site[None], env_local)


def solution(mesh):
    in_specs = (
        P("col", "tile", None, None),
        P("col", None, None, None, None),
        P("col", "tile", None),
        P("col", None, None, None),
        P("tile", None, None),
        P("col", None),
        P(),
    )
    out_specs = (P("col", "tile", None, None), P("col", "tile"))
    return jax.shard_map(local, mesh=mesh, in_specs=in_specs, out_specs=out_specs, check_vma=False)
```

```python
import functools

import jax
import jax.numpy as jnp
from jax import lax
from jax.experimental import pallas as pl
from jax.experimental.pallas import tpu as pltpu
from jax.sharding import PartitionSpec as P

GRAM_SHIFT = 0.001
NB = 128
OWNER = 0
SIDE = 4
HIGHEST = lax.Precision.HIGHEST
MESH = pl.DeviceIdType.MESH
VMEM = pl.BlockSpec(memory_space=pltpu.VMEM)


def f32_dot(x, y, dims=(((1,), (0,)), ((), ()))):
    return lax.dot_general(x, y, dims, precision=HIGHEST, preferred_element_type=jnp.float32)


def factor_block(block, inv_ref):
    sub = lax.broadcasted_iota(jnp.int32, (8, NB), 0)
    lane = lax.broadcasted_iota(jnp.int32, (8, NB), 1)
    a0 = tuple(block[8 * i:8 * i + 8, :] for i in range(16))
    m0 = tuple((lane == sub + 8 * i).astype(jnp.float32) for i in range(16))

    def along(x, t):
        return jnp.broadcast_to(x[:, t:t + 1], (8, NB))

    def down(x, t):
        return jnp.broadcast_to(x[t:t + 1, :], (8, NB))

    def tree(terms):
        while len(terms) > 1:
            terms = [terms[i] + terms[i + 1] for i in range(0, len(terms), 2)]
        return terms[0]

    def group(count, g, carry):
        a, m, c = list(carry[0]), list(carry[1]), list(carry[2])
        p, n = a[0], m[0]
        done = jnp.zeros((8, NB), jnp.float32)
        for s in range(8):
            here = sub == s
            pivot = down(c[s], s)
            inv = 1.0 / pivot
            nrow = down(n, s)
            done = jnp.where(here, nrow * lax.rsqrt(pivot), done)
            column = c[s]

            def step(x, row):
                row = row * inv
                return jnp.where(here, row, x - column * row)

            for t in range(s + 1, 8):
                c[t] = step(c[t], down(c[t], s))
            p = step(p, down(p, s))
            n = step(n, nrow)
        inv_ref[pl.ds(pl.multiple_of(g * 8, 8), 8), :] = done
        prow = [down(p, t) for t in range(8)]
        nrow = [down(n, t) for t in range(8)]
        for i in range(1, count):
            x = [along(a[i], t) for t in range(8)]
            a[i] = a[i] - tree([x[t] * prow[t] for t in range(8)])
            m[i] = m[i] - tree([x[t] * nrow[t] for t in range(8)])
            if i == 1:
                c = [along(a[1], 8 + t) for t in range(8)]
        zero = jnp.zeros((8, NB), jnp.float32)
        return tuple(pltpu.roll(x, NB - 8, 1) for x in a[1:]) + (zero,), tuple(m[1:]) + (zero,), tuple(c)

    carry = (a0, m0, tuple(along(a0[0], t) for t in range(8)))
    for lo in range(0, 16, 4):
        carry = (carry[0][:16 - lo], carry[1][:16 - lo], carry[2])
        carry = lax.fori_loop(lo, lo + 4, functools.partial(group, 16 - lo), carry)


class Place:
    def __init__(self):
        tile = lax.axis_index("tile")
        self.tile = tile
        self.y, self.x = tile // SIDE, tile % SIDE

    def coordinate(self, axis):
        return self.x if axis == 0 else self.y

    def along(self, axis, index):
        return self.y * SIDE + index if axis == 0 else index * SIDE + self.x


def remote(src, dst, send, recv, where):
    return pltpu.make_async_remote_copy(
        src_ref=src, dst_ref=dst, send_sem=send, recv_sem=recv, device_id=where, device_id_type=MESH)


class LineGather:
    def __init__(self, place, axis, own, slot, sems, row=None):
        self.place, self.axis, self.own, self.slot, self.row = place, axis, own, slot, row
        self.send1, self.recv1, self.send2, self.recv2 = sems

    def first(self, s):
        place = self.place
        target = place.along(self.axis, (place.coordinate(self.axis) + s) % SIDE)
        return remote(self.own, self.slot(place.tile), self.send1.at[s - 1], self.recv1.at[s - 1], {"tile": target})

    def second(self, s, j):
        place = self.place
        other = 1 - self.axis
        target = place.along(other, (place.coordinate(other) + s) % SIDE)
        source = place.along(self.axis, (place.coordinate(self.axis) + SIDE - j) % SIDE)
        piece = self.own if j == 0 else self.slot(source)
        return remote(piece, self.slot(source), self.send2.at[s - 1, j], self.recv2.at[s - 1, j], {"tile": target})

    def start(self):
        for s in range(1, SIDE):
            self.first(s).start()

    def forward(self):
        for s in range(1, SIDE):
            self.second(s, 0).start()
        for j in range(1, SIDE):
            self.first(j).wait_recv()
            for s in range(1, SIDE):
                self.second(s, j).start()

    def finish(self):
        for s in range(1, SIDE):
            for j in range(SIDE):
                self.second(s, j).wait_recv()
        for s in range(1, SIDE):
            self.first(s).wait_send()
            for j in range(SIDE):
                self.second(s, j).wait_send()


LINE_SEMS = [
    pltpu.SemaphoreType.DMA((2, SIDE - 1)),
    pltpu.SemaphoreType.DMA((2, SIDE - 1)),
    pltpu.SemaphoreType.DMA((2, SIDE - 1, SIDE)),
    pltpu.SemaphoreType.DMA((2, SIDE - 1, SIDE)),
]


def kernel(cols, tiles, b_ref, g_ref, amat_ref, h_ref, edge_ref, close_ref, first_ref, out_ref, env_ref, *scratch):
    (gall, r_ref, part, total, s_ref, inv_ref, kron_ref, phys_ref, q_ref, ball, qall, lall, qt, x1, yh, yl, acc, osend, oall,
     tsend, across, arrived, stage, landed) = scratch[:24]
    land, middle, land2, own = scratch[24:26], scratch[26:28], scratch[28:30], scratch[30:32]
    g_sems, b_sems = scratch[32:36], scratch[36:40]
    rs1_send, rs1_recv, rs2_send, rs2_recv, ag1_send, ag1_recv, ag2_send, ag2_recv, here_sem = scratch[40:49]
    (gather_send, gather_recv, chain_send, chain_recv, spread_send, spread_recv, keep_sem, q1_send, q1_recv, q2_send, q2_recv,
     l1_send, l1_recv, l2_send, l2_recv, o_send, o_recv, r_send, r_recv) = scratch[49:]
    place = Place()
    col = lax.axis_index("col")
    legs, share, width = b_ref.shape
    wide = width // SIDE
    first, last = col == 0, col == cols - 1
    barrier = pltpu.get_barrier_semaphore()

    def greet(where):
        pl.semaphore_signal(barrier, inc=1, device_id=where, device_id_type=MESH)

    for s in range(1, tiles):
        greet({"tile": (place.tile + s) % tiles})
    greet({"col": (col + cols - 1) % cols})
    pl.semaphore_wait(barrier, tiles)
    odd = col % 2
    k_step, c_step = SIDE - (SIDE - 1) * odd, 1 + (SIDE - 1) * odd
    k_index = place.y + (place.x - place.y) * odd
    c_index = place.x + (place.y - place.x) * odd

    def tile_of(k_block, c_block):
        return k_block * k_step + c_block * c_step

    half = share // 2
    sketch = [
        LineGather(
            place, h, g_ref.at[h * half:h * half + half],
            lambda tile, h=h: gall.at[pl.ds(pl.multiple_of(tile * share + h * half, half), half)],
            [x.at[h] for x in g_sems])
        for h in (0, 1)
    ]
    for gather in sketch:
        gather.start()
    mine = pl.multiple_of(place.tile * share, share)
    gall[pl.ds(mine, share), :] = g_ref[...]
    keep = pltpu.make_async_copy(b_ref, ball.at[:, pl.ds(mine, share), :], here_sem)
    keep.start()
    legs_sq = legs * legs
    spread_rows = lax.broadcasted_iota(jnp.int32, (16 * legs_sq, legs_sq), 0) // 16
    spread_cols = lax.broadcasted_iota(jnp.int32, (16 * legs_sq, legs_sq), 1)
    repeat = (spread_rows == spread_cols).astype(jnp.float32)
    mixed = f32_dot(f32_dot(repeat, amat_ref[...].T), repeat, (((1,), (1,)), ((), ())))
    same = (lax.broadcasted_iota(jnp.int32, mixed.shape, 0) % 16) == (lax.broadcasted_iota(jnp.int32, mixed.shape, 1) % 16)
    kron_ref[...] = jnp.where(same, mixed, 0.0).astype(jnp.bfloat16)
    phys_ref[...] = f32_dot(
        amat_ref[...], jnp.concatenate([h_ref[l].astype(jnp.float32) for l in range(legs)], axis=0))
    for gather in sketch:
        gather.forward()
    for gather in sketch:
        gather.finish()

    def chunk(ref, index):
        return ref.at[:, :, pl.ds(pl.multiple_of(index * wide, wide), wide)]

    def slot(ref, tile, count=1):
        return ref.at[:, pl.ds(pl.multiple_of(tile * share, share), count * share), :]

    def q1(s):
        target = (k_index + s) % SIDE
        return remote(chunk(q_ref, target), slot(qall, place.tile), q1_send.at[s - 1], q1_recv.at[s - 1],
                      {"tile": tile_of(target, c_index)})

    def q2(s, j):
        source = tile_of((k_index + SIDE - j) % SIDE, c_index)
        piece = chunk(q_ref, k_index) if j == 0 else slot(qall, source)
        return remote(piece, slot(qall, source), q2_send.at[s - 1, j], q2_recv.at[s - 1, j],
                      {"tile": tile_of(k_index, (c_index + s) % SIDE)})

    def right(s, j, column):
        source = tile_of((k_index + SIDE - j) % SIDE, (c_index + SIDE - s) % SIDE)
        piece = chunk(q_ref, k_index) if s == 0 and j == 0 else slot(qall, source)
        return remote(piece, slot(lall, source), r_send.at[s, j], r_recv.at[s, j], {"col": column})

    def pass_right(s, j):
        @pl.when(jnp.logical_not(last))
        def _():
            right(s, j, col + 1).start()

    def edge1(s):
        target = (place.x + s) % SIDE
        return remote(chunk(edge_ref, target), slot(lall, place.tile), l1_send.at[s], l1_recv.at[s],
                      {"tile": place.along(0, target)})

    def l2(s):
        rows = slot(lall, place.y * SIDE, SIDE)
        return remote(rows, rows, l2_send.at[s - 1], l2_recv.at[s - 1],
                      {"tile": place.along(1, (place.y + s) % SIDE)})

    def edge_own():
        return pltpu.make_async_copy(chunk(edge_ref, place.x), slot(lall, place.tile), l1_recv.at[0])

    def send_chunk(index):
        step = (index - k_index + SIDE) % SIDE

        @pl.when(step > 0)
        def _():
            q1(step).start()

    @pl.when(first)
    def _():
        edge_own().start()
        for s in range(1, SIDE):
            edge1(s).start()

    two = legs // 2
    sites = [
        LineGather(
            place, h, b_ref.at[h * two:h * two + two],
            lambda tile, h=h: ball.at[h * two:h * two + two, pl.ds(pl.multiple_of(tile * share, share), share), :],
            [x.at[h] for x in b_sems])
        for h in (0, 1)
    ]
    for gather in sites:
        gather.start()

    for u in range(legs):
        sketched = lax.dot_general(
            b_ref[u], gall[...], (((1,), (1,)), ((), ())), preferred_element_type=jnp.float32)
        for r in range(legs):
            term = sketched * phys_ref[u * legs + r:u * legs + r + 1, :]
            rows = slice(r * share, r * share + share)
            r_ref[rows, :] = term if u == 0 else r_ref[rows, :] + term

    blocks = width // NB
    pairs = blocks // 2
    packed = NB * (blocks + 1)
    cut = NB * (pairs + 1)
    columns = ((0, cut), (cut, packed))

    def view(ref, i):
        lo = 0 if i < pairs else (i + 1) * NB
        return ref.at[i if i < pairs else blocks - 1 - i, :, lo:lo + (blocks - i) * NB]

    flipped = r_ref[...].T
    strip = NB // SIDE

    def line(h):
        axis = h
        c1, c2 = place.coordinate(axis), place.coordinate(1 - axis)
        lo, hi = columns[h]
        return axis, c1, c2, slice(lo, hi)

    def rs1(h, s):
        axis, c1, c2, cols = line(h)
        p = (c1 + s) % SIDE
        return remote(part.at[p, :, cols], land[h].at[s - 1], rs1_send.at[h, s - 1], rs1_recv.at[h, s - 1],
                      {"tile": place.along(axis, p)})

    def rs2(h, s):
        axis, c1, c2, cols = line(h)
        p = (c2 + s) % SIDE
        return remote(middle[h].at[pl.ds(pl.multiple_of(p * strip, strip), strip)], land2[h].at[s - 1],
                      rs2_send.at[h, s - 1], rs2_recv.at[h, s - 1], {"tile": place.along(1 - axis, p)})

    def ag1(h, s):
        axis, c1, c2, cols = line(h)
        p = (c2 + s) % SIDE
        return remote(own[h], total.at[c1, pl.ds(pl.multiple_of(c2 * strip, strip), strip), cols],
                      ag1_send.at[h, s - 1], ag1_recv.at[h, s - 1], {"tile": place.along(1 - axis, p)})

    def ag2(h, s):
        axis, c1, c2, cols = line(h)
        p = (c1 + s) % SIDE
        return remote(total.at[c1, :, cols], total.at[c1, :, cols], ag2_send.at[h, s - 1], ag2_recv.at[h, s - 1],
                      {"tile": place.along(axis, p)})

    steps = range(1, SIDE)

    def send_pair(h, pair):
        step = (pair - place.coordinate(h) + SIDE) % SIDE

        @pl.when(step > 0)
        def _():
            rs1(h, step).start()

    for pair in range(pairs):
        for i in (pair, blocks - 1 - pair):
            view(part, i)[...] = f32_dot(flipped[i * NB:i * NB + NB, :], r_ref[:, i * NB:])
        for h in (0, 1):
            send_pair(h, pair)
    for h in (0, 1):
        axis, c1, c2, cols = line(h)
        for s in steps:
            rs1(h, s).wait_recv()
        middle[h][...] = ((part[c1, :, cols] + land[h][0]) + (land[h][1] + land[h][2]))
        for s in steps:
            rs2(h, s).start()
    for h in (0, 1):
        axis, c1, c2, cols = line(h)
        for s in steps:
            rs2(h, s).wait_recv()
        strip_rows = pl.ds(pl.multiple_of(c2 * strip, strip), strip)
        own[h][...] = ((middle[h][strip_rows, :] + land2[h][0]) + (land2[h][1] + land2[h][2]))
        for s in steps:
            ag1(h, s).start()
        total[c1, strip_rows, cols] = own[h][...]
    for h in (0, 1):
        for s in steps:
            ag1(h, s).wait_recv()
        for s in steps:
            ag2(h, s).start()
    for h in (0, 1):
        for s in steps:
            ag2(h, s).wait_recv()
    for h in (0, 1):
        for s in steps:
            for copy in (rs1, rs2, ag1, ag2):
                copy(h, s).wait_send()

    for gather in sites:
        gather.forward()

    eye = lax.broadcasted_iota(jnp.int32, (NB, NB), 0) == lax.broadcasted_iota(jnp.int32, (NB, NB), 1)
    for i in range(blocks):
        o, e = i * NB, i * NB + NB
        src = view(total, 0) if i == 0 else s_ref.at[o:e, o:]
        factor_block(src[:, :NB] + jnp.where(eye, GRAM_SHIFT, 0.0), inv_ref)
        inv = inv_ref[...]
        q = f32_dot(r_ref[:, o:e], inv, (((1,), (1,)), ((), ())))
        q_ref[:, :, o:e] = q.reshape(legs, share, NB).astype(q_ref.dtype)
        if e % wide == 0:
            send_chunk(e // wide - 1)
        if e == width:
            break
        upper = f32_dot(inv, src[:, NB:])
        r_ref[:, e:] = r_ref[:, e:] - f32_dot(q, upper)
        for k in range(i + 1, blocks):
            before = view(total, k)[...] if i == 0 else s_ref[k * NB:k * NB + NB, k * NB:]
            lo = (k - i - 1) * NB
            s_ref[k * NB:k * NB + NB, k * NB:] = before - f32_dot(upper[:, lo:lo + NB].T, upper[:, lo:])

    keep_q = pltpu.make_async_copy(chunk(q_ref, k_index), slot(qall, place.tile), keep_sem)
    keep_q.start()
    for s in steps:
        q2(s, 0).start()
    pass_right(0, 0)
    for j in steps:
        q1(j).wait_recv()
        for s in steps:
            q2(s, j).start()
        pass_right(0, j)

    @pl.when(first)
    def _():
        edge_own().wait()
        for s in steps:
            edge1(s).wait_recv()
        for s in steps:
            l2(s).start()

    keep_q.wait()
    for j in range(SIDE):
        for s in steps:
            q2(s, j).wait_recv()
            pass_right(s, j)
    part_k = wide // 2
    for r in range(legs):
        turned = qall[r].astype(jnp.float32).T.astype(jnp.bfloat16)
        for h in (0, 1):
            lo = (h * legs + r) * part_k
            qt[lo:lo + part_k, :] = turned[h * part_k:h * part_k + part_k]
    keep.wait()
    for gather in sites:
        gather.finish()

    def out(i):
        return remote(osend.at[i * wide:i * wide + wide],
                      oall.at[:, pl.ds(pl.multiple_of(c_index * wide, wide), wide)],
                      o_send.at[i], o_recv.at[c_index], {"tile": k_index * SIDE + i})

    def out_wait(c):
        return remote(osend.at[0:wide], oall.at[:, c * wide:c * wide + wide], o_send.at[0], o_recv.at[c], {"tile": OWNER})

    owner = place.tile == OWNER
    others = [t for t in range(tiles) if t != OWNER]

    def block(h):
        return (pl.ds(pl.multiple_of(c_index * wide, wide), wide),
                pl.ds(pl.multiple_of(k_index * wide + h * part_k, part_k), part_k))

    def gather(h, slot):
        return remote(tsend.at[h], across.at[block(h)], gather_send.at[h], gather_recv.at[h, slot], {"tile": OWNER})

    def spread(where):
        return remote(stage, landed, spread_send.at[where], spread_recv, {"tile": where})

    def chain(where):
        return remote(stage, arrived, chain_send, chain_recv, {"col": where})

    def scale_of(raw):
        squares = jnp.sum(raw * raw, axis=1, keepdims=True)
        return jnp.sqrt(jnp.float32(width)) / jnp.sqrt(squares + 1e-06)

    groups = part_k // 16
    unroll = 4
    for h in (0, 1):
        acc[...] = jnp.zeros_like(acc)
        base = h * legs * part_k

        @pl.loop(0, width // wide)
        def _(piece):
            lanes = pl.ds(pl.multiple_of(piece * wide, wide), wide)
            for u in range(legs):
                x1[:, u * wide:u * wide + wide] = jnp.dot(
                    qt[base:base + legs * part_k, :], ball[u, :, lanes], preferred_element_type=jnp.float32)

            @pl.loop(0, groups // unroll)
            def _(some):
                for g in [some * unroll + k for k in range(unroll)]:
                    start = pl.multiple_of(g * 16, 16)
                    stack = jnp.concatenate(
                        [x1[pl.ds(pl.multiple_of(r * part_k + start, 16), 16), u * wide:u * wide + wide]
                         for u in range(legs) for r in range(legs)], axis=0)
                    high = stack.astype(jnp.bfloat16)
                    low = (stack - high.astype(jnp.float32)).astype(jnp.bfloat16)
                    y = (jnp.dot(kron_ref[...], high, preferred_element_type=jnp.float32)
                         + jnp.dot(kron_ref[...], low, preferred_element_type=jnp.float32))
                    high = y.astype(jnp.bfloat16)
                    low = (y - high.astype(jnp.float32)).astype(jnp.bfloat16)
                    rows = pl.ds(pl.multiple_of(g * 64, 64), 64)
                    for l in range(legs):
                        yh[piece, l, rows, :] = high[l * 64:l * 64 + 64]
                        yl[piece, l, rows, :] = low[l * 64:l * 64 + 64]

        if h == 0:
            @pl.when(first)
            def _():
                for s in steps:
                    l2(s).wait_recv()

            @pl.when(jnp.logical_not(first))
            def _():
                for s in range(SIDE):
                    for j in range(SIDE):
                        right(s, j, col).wait_recv()

        @pl.loop(0, width // wide)
        def _(piece):
            lanes = pl.ds(pl.multiple_of(piece * wide, wide), wide)
            for l in range(legs):
                left = lall[l, lanes, :]
                term = (jnp.dot(yh[piece, l], left, preferred_element_type=jnp.float32)
                        + jnp.dot(yl[piece, l], left, preferred_element_type=jnp.float32))
                acc[...] = acc[...] + term

        osend[base:base + legs * part_k, :] = acc[...].astype(jnp.bfloat16)
        strips = []
        for g in range(groups):
            t = None
            for d in range(legs):
                lo = base + (g * legs + d) * 16
                term = osend[lo:lo + 16, :].astype(jnp.float32) * close_ref[0, d]
                t = term if t is None else t + term
            strips.append(t)
        transfer = jnp.concatenate(strips, axis=0).astype(jnp.bfloat16).astype(jnp.float32)
        tsend[h] = transfer.T.astype(jnp.bfloat16)

        @pl.when(jnp.logical_not(owner))
        def _():
            gather(h, place.tile).start()

    for i in range(SIDE):
        there = k_index * SIDE + i

        @pl.when(there != place.tile)
        def _():
            out(i).start()

        @pl.when(there == place.tile)
        def _():
            oall[:, pl.ds(pl.multiple_of(c_index * wide, wide), wide)] = osend[i * wide:i * wide + wide, :]

    @pl.when(owner)
    def _():
        for h in (0, 1):
            across[block(h)] = tsend[h]
            for t in others:
                gather(h, t).wait_recv()

        @pl.when(first)
        def _():
            arrived[...] = first_ref[...]

        @pl.when(jnp.logical_not(first))
        def _():
            chain(col).wait_recv()

        raw = arrived[...]
        high = raw.astype(jnp.bfloat16).astype(jnp.float32)
        middle = (raw - high).astype(jnp.bfloat16).astype(jnp.float32)
        low = raw - high - middle
        row = lax.broadcasted_iota(jnp.int32, (8, width), 0)
        parts = jnp.where(row == 0, high, jnp.where(row == 1, middle, jnp.where(row == 2, low, 0.0)))
        product = jnp.dot(parts.astype(jnp.bfloat16), across[...], preferred_element_type=jnp.float32)
        scale = jnp.where(first, 1.0, scale_of(raw))
        stage[...] = jnp.sum(product, axis=0, keepdims=True) * scale

        @pl.when(jnp.logical_not(last))
        def _():
            chain(col + 1).start()

        for t in others:
            spread(t).start()
        weighted = stage[...]
        env_ref[...] = weighted * scale_of(weighted)

    for c in range(SIDE):
        @pl.when(place.y * k_step + c * c_step != place.tile)
        def _():
            out_wait(c).wait_recv()

    out_ref[...] = oall[...]

    @pl.when(owner)
    def _():
        for t in others:
            spread(t).wait_send()

        @pl.when(jnp.logical_not(last))
        def _():
            chain(col + 1).wait_send()

    @pl.when(jnp.logical_not(owner))
    def _():
        spread(OWNER).wait_recv()
        weighted = landed[...]
        env_ref[...] = weighted * scale_of(weighted)
        for h in (0, 1):
            gather(h, place.tile).wait_send()

    for i in range(SIDE):
        @pl.when(k_index * SIDE + i != place.tile)
        def _():
            out(i).wait_send()

    for s in steps:
        q1(s).wait_send()
        for j in range(SIDE):
            q2(s, j).wait_send()

    @pl.when(first)
    def _():
        for s in steps:
            edge1(s).wait_send()
            l2(s).wait_send()

    @pl.when(jnp.logical_not(last))
    def _():
        for s in range(SIDE):
            for j in range(SIDE):
                right(s, j, col + 1).wait_send()


def absorb(site, sketch, amat, phys, edge, closing, left_edge, cols, tiles):
    legs, share, width = site.shape
    wide = width // SIDE
    packed = width + NB
    cut = NB * (width // NB // 2 + 1)
    sizes = (cut, packed - cut)
    strip = NB // SIDE
    bf16, f32 = jnp.bfloat16, jnp.float32
    dma = pltpu.SemaphoreType.DMA
    three = dma((2, SIDE - 1))
    vmem = pltpu.VMEM
    return pl.pallas_call(
        functools.partial(kernel, cols, tiles),
        out_shape=(
            jax.ShapeDtypeStruct((legs * share, width), bf16),
            jax.ShapeDtypeStruct((1, width), f32),
        ),
        in_specs=[VMEM] * 5 + [pl.BlockSpec(memory_space=pltpu.SMEM), VMEM],
        out_specs=(VMEM, VMEM),
        scratch_shapes=[
            vmem((width, width), bf16),
            vmem((legs * share, width), f32),
            vmem((SIDE, NB, packed), f32),
            vmem((SIDE, NB, packed), f32),
            vmem((width, width), f32),
            vmem((NB, NB), f32),
            vmem((16 * legs * legs, 16 * legs * legs), bf16),
            vmem((legs * legs, width), f32),
            vmem((legs, share, width), bf16),
            vmem((legs, width, width), bf16),
            vmem((legs, width, wide), bf16),
            vmem((legs, width, wide), bf16),
            vmem((legs * wide, width), bf16),
            vmem((legs * wide // 2, legs * wide), f32),
            vmem((SIDE, legs, legs * wide // 2, wide), bf16),
            vmem((SIDE, legs, legs * wide // 2, wide), bf16),
            vmem((legs * wide // 2, wide), f32),
            vmem((legs * wide, wide), bf16),
            vmem((legs * share, width), bf16),
            vmem((2, wide, wide // 2), bf16),
            vmem((width, width), bf16),
            vmem((1, width), f32),
            vmem((1, width), f32),
            vmem((1, width), f32),
            *[vmem((SIDE - 1, NB, size), f32) for size in sizes],
            *[vmem((NB, size), f32) for size in sizes],
            *[vmem((SIDE - 1, strip, size), f32) for size in sizes],
            *[vmem((strip, size), f32) for size in sizes],
            *LINE_SEMS,
            *LINE_SEMS,
            *[three] * 8,
            dma,
            dma((2,)), dma((2, tiles)), dma, dma, dma((tiles,)), dma,
            dma,
            dma((SIDE - 1,)), dma((SIDE - 1,)),
            dma((SIDE - 1, SIDE)), dma((SIDE - 1, SIDE)),
            dma((SIDE,)), dma((SIDE,)),
            dma((SIDE - 1,)), dma((SIDE - 1,)),
            dma((SIDE,)), dma((SIDE,)),
            dma((SIDE, SIDE)), dma((SIDE, SIDE)),
        ],
        compiler_params=pltpu.CompilerParams(collective_id=0, has_side_effects=True, vmem_limit_bytes=62 << 20),
    )(site, sketch, amat, phys, edge, closing, left_edge.reshape(1, width))


def local(boundary, row_tensors, sketch_bond, sketch_phys, edge_factor, closing, left_edge):
    cols, tiles = lax.axis_size("col"), lax.axis_size("tile")
    share, legs, width = boundary.shape[1:]
    amat = row_tensors[0].astype(jnp.float32).transpose(1, 2, 0, 3).reshape(legs * legs, legs * legs)
    rows, env = absorb(
        boundary[0].transpose(1, 0, 2), sketch_bond[0], amat, sketch_phys[0], edge_factor.transpose(1, 0, 2),
        closing, left_edge, cols, tiles)
    new_site = rows.reshape(share // 16, legs, 16, width).transpose(0, 2, 1, 3).reshape(share, legs, width)
    env_local = lax.dynamic_slice(env, (0, lax.axis_index("tile") * share), (1, share))
    return (new_site[None], env_local)


def solution(mesh):
    in_specs = (
        P("col", "tile", None, None),
        P("col", None, None, None, None),
        P("col", "tile", None),
        P("col", None, None, None),
        P("tile", None, None),
        P("col", None),
        P(),
    )
    out_specs = (P("col", "tile", None, None), P("col", "tile"))
    return jax.shard_map(local, mesh=mesh, in_specs=in_specs, out_specs=out_specs, check_vma=False)
```
